128 devices in a mesh: row: 16 (over y, z), col: 8 (over x, core).
Axes of the slice: x: 4, y: 4, z: 4, core: 2. Of those that a mesh axis runs over, the one named last changes fastest.
Arguments:
- child_parent: int32 [16384], P(('row', 'col')), may hold values from 0 to 4095, as said below
- prefix_len: int32 [16384], P(('row', 'col')), may hold values from 1 to 40
- child_delta: bfloat16 [16384, 3584], P(('row', 'col')), may hold values from -6 to 6
- parent_hidden: bfloat16 [4096, 3584], P(('row', 'col')), may hold values from -6 to 6
- parent_cache: bfloat16 [4096, 2, 2, 128, 128], P(('row', 'col')), may hold values from -720 to 720
- prefix_cache: bfloat16 [128, 2, 2, 5120, 128], P(('row', 'col')), may hold values from -720 to 720
- norm_gain: float32 [3584], replicated, may hold values from 0.1 to 1.9
- w_query: bfloat16 [3584, 1792], replicated, may hold values from -0.09375 to 0.09375
- w_kv: bfloat16 [3584, 512], replicated, may hold values from -0.09375 to 0.09375
Outputs:
- context: bfloat16 [16384, 1792], P(('row', 'col'))
- child_kv: bfloat16 [16384, 512], P(('row', 'col'))
The draws below stay inside these ranges and needn't reach their ends.
Inputs may be any that keep to these rules, and one draw needn't show every extreme that they name: `child_parent`: each device's 128 children name exactly 16 parents held in each column of devices; the children of any one row of devices name exactly 8 parents held by any one device; one device's children name at most 2 parents held by one device, and exactly 2 for some pairs. Parent p is held by device p // 32, device index = row index * 8 + column index.
All inputs are finite; a program needn't handle non-finite values.
Results may differ from the reference program's by a relative error of at most 0.0085.
The reference program's roundings to bfloat16 on the way count: a program that leaves them out, or rounds other values in their place, can miss the bound.
Values may be sent and summed in bfloat16 or wider, within the bound.
A program may use at most 256 MiB of HBM per device.

```python
import math
import jax
import jax.numpy as jnp
from jax import lax

D = 3584
QH = 14
KVH = 2
DH = 128
BLOCK = 128
PB = 40
C_DEV = 128
CHILDREN = 16384
PARENTS = 4096
N_ROW = 16
N_COL = 8


def draw_child_parent(key, part):
    device_count = N_ROW * N_COL
    half_span = C_DEV // (2 * N_COL)
    shift_reach = half_span % N_ROW if half_span % N_ROW else N_ROW
    key_shift, key_rows, key_cols, key_slots, key_local = jax.random.split(jax.random.fold_in(key, 11), 5)
    offsets = jnp.arange(half_span, dtype=jnp.int32)
    start_rows = jnp.arange(N_COL, dtype=jnp.int32)[:, None] * half_span
    base_rows = (start_rows + offsets[None, :]) % N_ROW
    shift_draw = jax.random.randint(key_shift, (N_ROW, N_COL, 1, 1), 0, shift_reach)
    first_cover = jnp.broadcast_to(base_rows, (N_ROW, N_COL, N_COL, half_span))
    second_cover = (first_cover + shift_draw) % N_ROW
    source_rows = jnp.concatenate([first_cover, second_cover], axis=3)
    row_order = jax.vmap(lambda one_key: jax.random.permutation(one_key, N_ROW))(jax.random.split(key_rows, N_ROW * N_COL))
    row_order = jnp.broadcast_to(row_order.reshape(N_ROW, N_COL, 1, N_ROW), (N_ROW, N_COL, N_COL, N_ROW))
    source_rows = jnp.take_along_axis(row_order, source_rows, axis=3)
    col_order = jax.vmap(lambda one_key: jax.random.permutation(one_key, N_COL))(jax.random.split(key_cols, N_ROW * N_COL))
    col_inverse = jnp.argsort(col_order.reshape(N_ROW, N_COL, N_COL), axis=-1).astype(jnp.int32)
    col_inverse = jnp.broadcast_to(col_inverse[..., None], (N_ROW, N_COL, N_COL, 2 * half_span))
    source_rows = jnp.take_along_axis(source_rows, col_inverse, axis=2)
    source_dev = source_rows * N_COL + jnp.arange(N_COL, dtype=jnp.int32)[None, :, None, None]
    source_dev = jnp.transpose(source_dev, (0, 2, 1, 3)).reshape(device_count, C_DEV)
    slot_order = jax.vmap(lambda one_key: jax.random.permutation(one_key, C_DEV))(jax.random.split(key_slots, device_count))
    source_dev = jnp.take_along_axis(source_dev, slot_order, axis=1)
    local_ids = jax.random.randint(key_local, (device_count, C_DEV), 0, C_DEV // 4)
    return (source_dev * (C_DEV // 4) + local_ids).reshape(device_count * C_DEV).astype(jnp.int32)


def spiked_draw(key, shape):
    key_base = jax.random.fold_in(key, 0)
    normal_part = jnp.clip(jax.random.normal(key_base, shape, jnp.float32), -6.0, 6.0)
    return normal_part.astype(jnp.bfloat16)


def draw_parent_cache(key, part):
    return spiked_draw(jax.random.fold_in(key, 31), (C_DEV // 4 * N_ROW * N_COL, 2, KVH, BLOCK, DH))


def draw_prefix_cache(key, part):
    return spiked_draw(jax.random.fold_in(key, 21), (N_ROW * N_COL, 2, KVH, PB * BLOCK, DH))


def set_ends(array, stream_key, least, largest):
    extent = array.shape
    spot = [jax.random.randint(jax.random.fold_in(stream_key, axis), (), 0, extent[axis]) for axis in range(len(extent))]
    array = array.at[tuple(spot)].set(least)
    longest = extent.index(max(extent))
    spot[longest] = (spot[longest] + 1) % extent[longest]
    return array.at[tuple(spot)].set(largest)


def block_levels(own_key, extent, cuts, smallest, largest):
    factor_of, own = 1.0, jax.random.fold_in(own_key, 6)
    for position, parts in cuts:
        draws = jnp.exp(jax.random.uniform(jax.random.fold_in(own, position), (parts,), jnp.float32, smallest / len(cuts), largest / len(cuts)))
        factor_of = factor_of * jnp.repeat(draws, extent[position] // parts).reshape([-1 if axis == position else 1 for axis in range(len(extent))])
    return factor_of


def gaussian(own_key, extent, deviation, limit, pieces=(), kind=jnp.bfloat16):
    array = deviation * jax.random.normal(own_key, extent, jnp.float32)
    if pieces:
        array = array * block_levels(own_key, extent, pieces, -0.22, 0.18)
    return jnp.clip(array, -limit, limit).astype(kind)


def setup_inputs(seed: int = 0) -> dict:
    splits = jax.random.split(jax.random.key(seed), 10)
    return {
        "child_parent": draw_child_parent(jax.random.fold_in(splits[9], 71), 0),
        "prefix_len": set_ends(jax.random.randint(splits[1], (CHILDREN,), 1, PB + 1), jax.random.fold_in(splits[1], 1), 1, PB).astype(jnp.int32),
        "child_delta": gaussian(splits[2], (CHILDREN, D), 1.0, 6.0, ((0, 128),)),
        "parent_hidden": gaussian(splits[3], (PARENTS, D), 1.0, 6.0, ((0, 128),)),
        "parent_cache": draw_parent_cache(jax.random.fold_in(splits[9], 71), 0),
        "prefix_cache": draw_prefix_cache(jax.random.fold_in(splits[9], 71), 0),
        "norm_gain": jnp.clip(1.0 + 0.18 * jax.random.normal(splits[6], (D,), jnp.float32), 0.1, 1.9),
        "w_query": gaussian(splits[7], (D, QH * DH), D ** -0.5, 0.09375),
        "w_kv": gaussian(splits[8], (D, 2 * KVH * DH), D ** -0.5, 0.09375),
    }


EPSILON = 1e-06

def decode_child(parent_rows, parent_blocks, delta_rows, block_counts, prefix_rows, norm_gain, w_query, w_kv):
    highest = lax.Precision.HIGHEST
    widened = parent_rows.astype(jnp.float32) + delta_rows.astype(jnp.float32)
    inverse = lax.rsqrt(lax.optimization_barrier(jnp.mean(widened * widened, axis=-1, keepdims=True)) + EPSILON)
    normed = (widened * inverse * norm_gain).astype(jnp.bfloat16)
    queries = jnp.dot(normed, w_query, preferred_element_type=jnp.float32).astype(jnp.bfloat16)
    new_kv = jnp.dot(normed, w_kv, preferred_element_type=jnp.float32).astype(jnp.bfloat16)
    child_count = parent_rows.shape[0]
    kv_heads = prefix_rows.shape[1]
    head_dim = prefix_rows.shape[-1]
    block_tokens = parent_blocks.shape[3]
    grouped = queries.astype(jnp.float32).reshape(child_count, kv_heads, -1, head_dim)
    scale_factor = 1.0 / math.sqrt(head_dim)
    prefix_keys = prefix_rows[0].astype(jnp.float32)
    score_pre = jnp.einsum('chgd,hld->hcgl', grouped, prefix_keys, precision=highest) * scale_factor
    key_positions = jnp.arange(prefix_keys.shape[1], dtype=jnp.int32)
    limits = block_counts * block_tokens
    in_prefix = key_positions[None, None, None, :] < limits[None, :, None, None]
    score_pre = jnp.where(in_prefix, score_pre, -jnp.inf)
    score_par = jnp.einsum('chgd,chtd->hcgt', grouped, parent_blocks[:, 0].astype(jnp.float32), precision=highest) * scale_factor
    top_score = jnp.maximum(lax.optimization_barrier(jnp.max(score_pre, axis=-1, keepdims=True)), lax.optimization_barrier(jnp.max(score_par, axis=-1, keepdims=True)))
    exp_pre = jnp.exp(score_pre - top_score)
    exp_par = jnp.exp(score_par - top_score)
    denominator = lax.optimization_barrier(jnp.sum(exp_pre, axis=-1, keepdims=True)) + lax.optimization_barrier(jnp.sum(exp_par, axis=-1, keepdims=True))
    weight_pre = (exp_pre / denominator).astype(jnp.bfloat16)
    weight_par = (exp_par / denominator).astype(jnp.bfloat16)
    context = jnp.einsum('hcgl,hld->chgd', weight_pre.astype(jnp.float32), prefix_rows[1].astype(jnp.float32), precision=highest)
    context = context + jnp.einsum('hcgt,chtd->chgd', weight_par.astype(jnp.float32), parent_blocks[:, 1].astype(jnp.float32), precision=highest)
    return (context.reshape(child_count, -1).astype(jnp.bfloat16), new_kv)

def reference(child_parent, prefix_len, child_delta, parent_hidden, parent_cache, prefix_cache, norm_gain, w_query, w_kv):

    def per_device(device):
        first_child = device * C_DEV
        parent_ids = lax.dynamic_slice_in_dim(child_parent, first_child, C_DEV, 0)
        block_counts = lax.dynamic_slice_in_dim(prefix_len, first_child, C_DEV, 0)
        delta_rows = lax.dynamic_slice_in_dim(child_delta, first_child, C_DEV, 0)
        prefix_rows = lax.dynamic_index_in_dim(prefix_cache, device, 0, keepdims=False)
        return decode_child(parent_hidden[parent_ids], parent_cache[parent_ids], delta_rows, block_counts, prefix_rows, norm_gain, w_query, w_kv)
    context, new_kv = lax.map(per_device, jnp.arange(N_ROW * N_COL, dtype=jnp.int32))
    return (context.reshape(CHILDREN, -1), new_kv.reshape(CHILDREN, -1))
```

```python
import functools
import math

import jax
import jax.numpy as jnp
from jax import lax
from jax.experimental import pallas as pl
from jax.experimental.pallas import tpu as pltpu
from jax.sharding import PartitionSpec as P

EPSILON = 1e-06
F32 = jnp.float32
BF16 = jnp.bfloat16
I32 = jnp.int32
ROWS = 16
COLS = 8
N = 128
D = 3584
HEADS = 14
GROUP = 7
DH = 128
PARENTS = 32
BLOCK = 128
DELTA_CHUNKS = 2
CHUNK = D // DELTA_CHUNKS
HALF = CHUNK // 2
BACK_CHUNKS = 3
SHARE_CHUNKS = 2
TILE = 32
KEYS = 512
SCORE_SCALE = math.log2(math.e) / math.sqrt(DH)


def iotas(shape):
    return lax.broadcasted_iota(I32, shape, 0), lax.broadcasted_iota(I32, shape, 1)


def one_zero(mask, kind=BF16):
    return jnp.where(mask, 1.0, 0.0).astype(kind)


def to_col(row):
    below, along = iotas((N, N))
    return jnp.sum(jnp.where(below == along, row, 0.0), axis=1, keepdims=True)


def to_row(col):
    below, along = iotas((N, N))
    return jnp.sum(jnp.where(below == along, col, 0.0), axis=0, keepdims=True)


def rank_row(key_row, key_col):
    below, along = iotas((N, N))
    earlier = (key_col == key_row) & (below < along)
    return jnp.sum(jnp.where(earlier, 1.0, 0.0), axis=0, keepdims=True)


def column_order(ids):
    column = ((ids >> 5) & (COLS - 1)).astype(F32)
    return column * 16.0 + rank_row(column, to_col(column))


def dot(a, b):
    return jnp.dot(a, b, preferred_element_type=F32)


def dot_t(a, b):
    return lax.dot_general(a, b, (((1,), (1,)), ((), ())), preferred_element_type=F32)


def pair_rows(left, right):
    width = left.shape[1]
    both = jnp.concatenate(
        [left.reshape(ROWS, 1, 8, width), right.reshape(ROWS, 1, 8, width)], axis=1
    )
    return both.reshape(2 * N, width)


class Exchange:
    def __init__(self, axis, count, me, rows):
        self.axis, self.count, self.me, self.rows = axis, count, me, rows

    def part(self, ref, k):
        return ref.at[pl.ds(pl.multiple_of(k * self.rows, self.rows), self.rows)]

    def copy(self, src, dst, send, recv, k, slot):
        return pltpu.make_async_remote_copy(
            src_ref=self.part(src, k),
            dst_ref=self.part(dst, slot),
            send_sem=send.at[k],
            recv_sem=recv.at[slot],
            device_id={self.axis: k},
            device_id_type=pl.DeviceIdType.MESH,
        )

    def each(self, act):
        def body(k, carry):
            act(lax.rem(self.me + k, self.count))
            return carry

        lax.fori_loop(1, self.count, body, 0)

    def start(self, src, dst, send, recv):
        self.each(lambda k: self.copy(src, dst, send, recv, k, self.me).start())
        own = pl.ds(pl.multiple_of(self.me * self.rows, self.rows), self.rows)
        dst[own, :] = src[own, :]

    def arrived(self, src, dst, send, recv):
        self.each(lambda k: self.copy(src, dst, send, recv, k, k).wait_recv())

    def sent(self, src, dst, send, recv):
        self.each(lambda k: self.copy(src, dst, send, recv, k, self.me).wait_send())


def parent_kernel(
    ids_ref,
    gain_ref,
    delta_hbm,
    hidden_hbm,
    blocks_hbm,
    wq_hbm,
    wkv_hbm,
    back_ref,
    share_ref,
    delta_v,
    hidden_v,
    blocks_v,
    weight_v,
    out1,
    in1,
    out2,
    in2,
    id_out1,
    id_in1,
    id_out2,
    id_in2,
    wide,
    normed,
    heads_v,
    back1,
    back1_in,
    back2,
    score,
    total,
    prob,
    stat,
    share1,
    share1_in,
    share2,
    load_sem,
    d1s,
    d1r,
    d2s,
    d2r,
    i1s,
    i1r,
    i2s,
    i2r,
    b1s,
    b1r,
    b2s,
    b2r,
    s1s,
    s1r,
    s2s,
    s2r,
):
    my_row = lax.axis_index("row")
    my_col = lax.axis_index("col")
    load_delta = pltpu.make_async_copy(delta_hbm, delta_v, load_sem.at[0])
    load_delta.start()

    barrier = pltpu.get_barrier_semaphore()

    def greet_col(k, carry):
        pl.semaphore_signal(
            barrier,
            inc=1,
            device_id={"col": lax.rem(my_col + k, COLS)},
            device_id_type=pl.DeviceIdType.MESH,
        )
        return carry

    def greet_row(k, carry):
        pl.semaphore_signal(
            barrier,
            inc=1,
            device_id={"row": lax.rem(my_row + k, ROWS)},
            device_id_type=pl.DeviceIdType.MESH,
        )
        return carry

    lax.fori_loop(1, COLS, greet_col, 0)
    lax.fori_loop(1, ROWS, greet_row, 0)

    below, along = iotas((N, N))
    ids = ids_ref[...]
    order = column_order(ids)
    pick = order == below.astype(F32)
    sorting = one_zero(pick)
    far_row = (ids >> 8).astype(F32)
    far_local = (ids & (PARENTS - 1)).astype(F32)
    row_sorted = jnp.sum(jnp.where(pick, far_row, 0.0), axis=1, keepdims=True)
    local_sorted = jnp.sum(jnp.where(pick, far_local, 0.0), axis=1, keepdims=True)
    id_out1[...] = jnp.where(along < 64, row_sorted, local_sorted).astype(BF16)

    load_delta.wait()
    loads = [
        pltpu.make_async_copy(hidden_hbm, hidden_v, load_sem.at[1]),
        pltpu.make_async_copy(wq_hbm, weight_v.at[:, pl.ds(0, HEADS * DH)], load_sem.at[2]),
        pltpu.make_async_copy(wkv_hbm, weight_v.at[:, pl.ds(HEADS * DH, 512)], load_sem.at[3]),
        pltpu.make_async_copy(blocks_hbm, blocks_v, load_sem.at[4]),
    ]

    by_col = Exchange("col", COLS, my_col, 16)
    by_row = Exchange("row", ROWS, my_row, 16)
    by_row8 = Exchange("row", ROWS, my_row, 8)

    pl.semaphore_wait(barrier, COLS + ROWS - 2)
    by_col.start(id_out1, id_in1, i1s, i1r)
    for c in range(DELTA_CHUNKS):
        out1[c] = dot(sorting, delta_v[:, c * CHUNK : (c + 1) * CHUNK]).astype(BF16)
        by_col.start(out1.at[c], in1.at[c], d1s.at[c], d1r.at[c])
    for load in loads:
        load.start()

    by_col.arrived(id_out1, id_in1, i1s, i1r)
    arrived_ids = id_in1[...].astype(F32)
    row_col = arrived_ids[:, 0:1]
    row_row = to_row(row_col)
    local_row = to_row(arrived_ids[:, 64:65])
    place = row_row * 8.0 + rank_row(row_row, row_col)
    place_col = to_col(place)
    place_pick = place == below.astype(F32)
    id_out2[...] = jnp.broadcast_to(
        jnp.sum(jnp.where(place_pick, local_row, 0.0), axis=1, keepdims=True), (N, N)
    )
    by_row8.start(id_out2, id_in2, i2s, i2r)

    wide_below, wide_along = iotas((2 * N, 2 * N))
    code_below = ((wide_below >> 4) * 16 + (wide_below & 7) * 2 + ((wide_below >> 3) & 1)).astype(
        F32
    )
    code_along = ((wide_along >> 4) * 16 + (wide_along & 7) * 2 + ((wide_along >> 3) & 1)).astype(
        F32
    )
    code_row = jnp.concatenate([place * 2.0, place * 2.0 + 1.0], axis=1)
    code_col = jnp.concatenate([place_col * 2.0, place_col * 2.0 + 1.0], axis=0)
    forth = one_zero(code_below == code_row)
    turn = one_zero(code_along == code_col)

    for c in range(DELTA_CHUNKS):
        by_col.arrived(out1.at[c], in1.at[c], d1s.at[c], d1r.at[c])
        stacked = jnp.concatenate([in1[c, :, :HALF], in1[c, :, HALF:]], axis=0)
        out2[c] = dot(forth, stacked).astype(BF16)
        by_row.start(out2.at[c], in2.at[c], d2s.at[c], d2r.at[c])

    loads[0].wait()
    by_row8.arrived(id_out2, id_in2, i2s, i2r)
    local_id = id_in2[...]
    owner = one_zero(local_id[:, :PARENTS] == along[:, :PARENTS].astype(F32))
    squares = jnp.zeros((N, 1), F32)
    for c in range(DELTA_CHUNKS):
        by_row.arrived(out2.at[c], in2.at[c], d2s.at[c], d2r.at[c])
        for half in range(2):
            for w in range(HALF // 128):
                at = c * CHUNK + half * HALF + w * 128
                grid = in2[c, :, w * 128 : (w + 1) * 128].astype(F32)
                grid = grid.reshape(ROWS, 2, 8, 128)[:, half].reshape(N, 128)
                value = dot(owner, hidden_v[:, at : at + 128]) + grid
                wide[:, at : at + 128] = value
                squares = squares + jnp.sum(value * value, axis=1, keepdims=True)
    inverse = lax.rsqrt(squares / D + EPSILON)
    for w in range(D // 128):
        at = w * 128
        normed[:, at : at + 128] = (
            wide[:, at : at + 128] * inverse * gain_ref[:, at : at + 128]
        ).astype(BF16)

    loads[1].wait()
    loads[2].wait()
    for c in range(BACK_CHUNKS):

        def project(t, carry, c=c):
            n = c * 3 + t
            y = dot(normed[...], weight_v[:, pl.ds(pl.multiple_of(n * 256, 256), 256)])
            heads_v[2 * n] = y[:, :128].astype(BF16)
            heads_v[2 * n + 1] = y[:, 128:].astype(BF16)
            back1[c, :, pl.ds(pl.multiple_of(t * 128, 128), 128)] = pair_rows(
                y[:, :128], y[:, 128:]
            ).astype(BF16)
            return carry

        lax.fori_loop(0, 3, project, 0)
        by_row.start(back1.at[c], back1_in.at[c], b1s.at[c], b1r.at[c])

    loads[3].wait()
    score[...] = jnp.zeros_like(score)
    total[...] = jnp.zeros_like(total)

    def masks(k):
        first = (2 * k).astype(F32)
        return one_zero(local_id == first), one_zero(local_id == first + 1.0)

    def score_pair(k, carry):
        mask0, mask1 = masks(k)
        for g in range(2):
            keys = jnp.concatenate([blocks_v[2 * k, 0, g], blocks_v[2 * k + 1, 0, g]], axis=1)
            for h in range(g * GROUP, (g + 1) * GROUP):
                q = heads_v[h]
                score[h] += dot_t(jnp.concatenate([q * mask0, q * mask1], axis=1), keys)
        return carry

    lax.fori_loop(0, PARENTS // 2, score_pair, 0)

    for c in range(BACK_CHUNKS):
        by_row.arrived(back1.at[c], back1_in.at[c], b1s.at[c], b1r.at[c])
        turned = dot(turn, back1_in[c]).astype(BF16)
        for t in range(3):
            back2[c, :, t * 256 : t * 256 + 128] = turned[:N, t * 128 : (t + 1) * 128]
            back2[c, :, t * 256 + 128 : (t + 1) * 256] = turned[N:, t * 128 : (t + 1) * 128]
        by_col.start(back2.at[c], back_ref.at[c], b2s.at[c], b2r.at[c])

    for g in range(2):
        stats = jnp.zeros((N, N), F32)
        for h in range(GROUP):
            s = score[g * GROUP + h] * SCORE_SCALE
            top = jnp.max(s, axis=1, keepdims=True)
            e = jnp.exp2(s - top)
            prob[g * GROUP + h] = e.astype(BF16)
            stats = jnp.where(along == h, top, stats)
            stats = jnp.where(along == 8 + h, jnp.sum(e, axis=1, keepdims=True), stats)
        stat[g] = stats

    def value_pair(k, carry):
        mask0, mask1 = masks(k)
        for g in range(2):
            values = jnp.concatenate([blocks_v[2 * k, 1, g], blocks_v[2 * k + 1, 1, g]], axis=0)
            for h in range(g * GROUP, (g + 1) * GROUP):
                p = prob[h]
                total[h] += dot(jnp.concatenate([p * mask0, p * mask1], axis=1), values)
        return carry

    lax.fori_loop(0, PARENTS // 2, value_pair, 0)

    for c in range(SHARE_CHUNKS):
        for b in range(4):
            h = c * 4 + b
            sides = []
            for g in range(2):
                stats = stat[g]
                if h < GROUP:
                    sides.append(total[g * GROUP + h] / stats[:, 8 + h : 9 + h])
                else:
                    high = stats.astype(BF16).astype(F32)
                    rest = stats - high
                    middle = rest.astype(BF16).astype(F32)
                    low = rest - middle
                    sides.append(
                        high + pltpu.roll(middle, shift=16, axis=1) + pltpu.roll(low, shift=32, axis=1)
                    )
            share1[c, :, b * 128 : (b + 1) * 128] = pair_rows(sides[0], sides[1]).astype(BF16)
        by_row.start(share1.at[c], share1_in.at[c], s1s.at[c], s1r.at[c])

    for c in range(SHARE_CHUNKS):
        by_row.arrived(share1.at[c], share1_in.at[c], s1s.at[c], s1r.at[c])
        turned = dot(turn, share1_in[c]).astype(BF16)
        share2[c, :, :512] = turned[:N]
        share2[c, :, 512:] = turned[N:]
        by_col.start(share2.at[c], share_ref.at[c], s2s.at[c], s2r.at[c])

    for c in range(BACK_CHUNKS):
        by_col.arrived(back2.at[c], back_ref.at[c], b2s.at[c], b2r.at[c])
    for c in range(SHARE_CHUNKS):
        by_col.arrived(share2.at[c], share_ref.at[c], s2s.at[c], s2r.at[c])

    by_col.sent(id_out1, id_in1, i1s, i1r)
    by_row8.sent(id_out2, id_in2, i2s, i2r)
    for c in range(DELTA_CHUNKS):
        by_col.sent(out1.at[c], in1.at[c], d1s.at[c], d1r.at[c])
        by_row.sent(out2.at[c], in2.at[c], d2s.at[c], d2r.at[c])
    for c in range(BACK_CHUNKS):
        by_row.sent(back1.at[c], back1_in.at[c], b1s.at[c], b1r.at[c])
        by_col.sent(back2.at[c], back_ref.at[c], b2s.at[c], b2r.at[c])
    for c in range(SHARE_CHUNKS):
        by_row.sent(share1.at[c], share1_in.at[c], s1s.at[c], s1r.at[c])
        by_col.sent(share2.at[c], share_ref.at[c], s2s.at[c], s2r.at[c])


def prefix_kernel(
    ids_ref,
    lens_ref,
    back_ref,
    share_ref,
    prefix_hbm,
    context_ref,
    kv_ref,
    keys_v,
    values_v,
    query_v,
    part_v,
    stat_v,
    result_v,
    top,
    mass,
    total,
    load_sem,
):
    loads = []
    for g in range(2):
        loads.append(
            pltpu.make_async_copy(prefix_hbm.at[0, g], keys_v.at[g], load_sem.at[2 * g])
        )
        loads.append(
            pltpu.make_async_copy(prefix_hbm.at[1, g], values_v.at[g], load_sem.at[2 * g + 1])
        )
    for load in loads:
        load.start()

    below, along = iotas((N, N))
    along_f = along.astype(F32)
    below_f = below.astype(F32)
    arrive_col = to_col(column_order(ids_ref[...]))
    lens = lens_ref[...].astype(F32)
    lens_col = to_col(lens)
    before = (lens_col > lens) | ((lens_col == lens) & (below < along))
    place = jnp.sum(jnp.where(before, 1.0, 0.0), axis=0, keepdims=True)
    place_col = to_col(place)
    unsort1 = one_zero(arrive_col == along_f)
    pick = place == below_f
    gather = dot(one_zero(pick), unsort1).astype(BF16)
    sorted_lens = jnp.sum(jnp.where(pick, lens, 0.0), axis=1, keepdims=True)

    for n in range(GROUP):
        c, t = n // 3, n % 3
        query_v[:, n * 256 : (n + 1) * 256] = dot(
            gather, back_ref[c, :, t * 256 : (t + 1) * 256]
        ).astype(BF16)
    for n in range(2):
        kv_ref[:, n * 256 : (n + 1) * 256] = dot(
            unsort1, back_ref[2, :, (n + 1) * 256 : (n + 2) * 256]
        ).astype(BF16)
    for g in range(2):
        for h in range(GROUP):
            c, b = h // 4, h % 4
            part_v[:, (g * GROUP + h) * 128 : (g * GROUP + h + 1) * 128] = dot(
                gather, share_ref[c, :, g * 512 + b * 128 : g * 512 + (b + 1) * 128]
            )
        packed = dot(gather, share_ref[1, :, g * 512 + 384 : g * 512 + 512])
        stat_v[g] = (
            packed
            + pltpu.roll(packed, shift=N - 16, axis=1)
            + pltpu.roll(packed, shift=N - 32, axis=1)
        )

    for g in range(2):
        loads[2 * g].wait()
        loads[2 * g + 1].wait()
        for t in range(N // TILE):
            rows = slice(t * TILE, (t + 1) * TILE)
            limit = jnp.concatenate([sorted_lens[rows] * float(BLOCK)] * GROUP, axis=0)
            longest = jnp.max(sorted_lens[rows]).astype(I32)
            steps = (longest * BLOCK + KEYS - 1) // KEYS
            q = jnp.concatenate(
                [
                    query_v[rows, (g * GROUP + h) * 128 : (g * GROUP + h + 1) * 128]
                    for h in range(GROUP)
                ],
                axis=0,
            )
            top[...] = jnp.full_like(top, -jnp.inf)
            mass[...] = jnp.zeros_like(mass)
            total[...] = jnp.zeros_like(total)

            def step(j, carry, g=g, q=q, limit=limit):
                start = pl.multiple_of(j * KEYS, KEYS)
                s = dot_t(q, keys_v[g, pl.ds(start, KEYS), :]) * SCORE_SCALE
                spot = lax.broadcasted_iota(I32, s.shape, 1).astype(F32) + start.astype(F32)
                s = jnp.where(spot < limit, s, -jnp.inf)
                old = top[...]
                new = jnp.maximum(old, jnp.max(s, axis=1, keepdims=True))
                p = jnp.exp2(s - new)
                shrink = jnp.exp2(old - new)
                mass[...] = mass[...] * shrink + jnp.sum(p, axis=1, keepdims=True)
                total[...] = total[...] * shrink + dot(
                    p.astype(BF16), values_v[g, pl.ds(start, KEYS), :]
                )
                top[...] = new
                return carry

            lax.fori_loop(0, steps, step, 0)
            stats = stat_v[g, rows]
            for h in range(GROUP):
                at = (g * GROUP + h) * 128
                own = slice(h * TILE, (h + 1) * TILE)
                top_par = stats[:, h : h + 1]
                mass_par = stats[:, 8 + h : 9 + h]
                top_all = jnp.maximum(top[own], top_par)
                near = jnp.exp2(top[own] - top_all)
                far = jnp.exp2(top_par - top_all) * mass_par
                whole = mass[own] * near + far
                result_v[rows, at : at + 128] = (
                    (total[own] * near + part_v[rows, at : at + 128] * far) / whole
                ).astype(BF16)

    unsort = one_zero(place_col == along_f)
    for n in range(GROUP):
        context_ref[:, n * 256 : (n + 1) * 256] = dot(
            unsort, result_v[:, n * 256 : (n + 1) * 256]
        ).astype(BF16)


def local(
    child_parent,
    prefix_len,
    child_delta,
    parent_hidden,
    parent_cache,
    prefix_cache,
    norm_gain,
    w_query,
    w_kv,
):
    vmem = pl.BlockSpec(memory_space=pltpu.VMEM)
    hbm = pl.BlockSpec(memory_space=pl.ANY)
    dma = pltpu.SemaphoreType.DMA
    ids = child_parent.reshape(1, N)
    lens = prefix_len.reshape(1, N)
    back_shape = (BACK_CHUNKS, N, 768)
    share_shape = (SHARE_CHUNKS, N, 1024)
    back, share = pl.pallas_call(
        parent_kernel,
        name="parent_side",
        out_shape=(
            jax.ShapeDtypeStruct(back_shape, BF16),
            jax.ShapeDtypeStruct(share_shape, BF16),
        ),
        in_specs=[vmem, vmem, hbm, hbm, hbm, hbm, hbm],
        out_specs=(vmem, vmem),
        scratch_shapes=[
            pltpu.VMEM((N, D), BF16),
            pltpu.VMEM((PARENTS, D), BF16),
            pltpu.VMEM((PARENTS, 2, 2, BLOCK, DH), BF16),
            pltpu.VMEM((D, 2304), BF16),
            pltpu.VMEM((DELTA_CHUNKS, N, CHUNK), BF16),
            pltpu.VMEM((DELTA_CHUNKS, N, CHUNK), BF16),
            pltpu.VMEM((DELTA_CHUNKS, 2 * N, HALF), BF16),
            pltpu.VMEM((DELTA_CHUNKS, 2 * N, HALF), BF16),
            pltpu.VMEM((N, N), BF16),
            pltpu.VMEM((N, N), BF16),
            pltpu.VMEM((N, N), F32),
            pltpu.VMEM((N, N), F32),
            pltpu.VMEM((N, D), F32),
            pltpu.VMEM((N, D), BF16),
            pltpu.VMEM((18, N, 128), BF16),
            pltpu.VMEM((BACK_CHUNKS, 2 * N, 384), BF16),
            pltpu.VMEM((BACK_CHUNKS, 2 * N, 384), BF16),
            pltpu.VMEM(back_shape, BF16),
            pltpu.VMEM((HEADS, N, BLOCK), F32),
            pltpu.VMEM((HEADS, N, DH), F32),
            pltpu.VMEM((HEADS, N, BLOCK), BF16),
            pltpu.VMEM((2, N, N), F32),
            pltpu.VMEM((SHARE_CHUNKS, 2 * N, 512), BF16),
            pltpu.VMEM((SHARE_CHUNKS, 2 * N, 512), BF16),
            pltpu.VMEM(share_shape, BF16),
            dma((5,)),
            dma((DELTA_CHUNKS, COLS)),
            dma((DELTA_CHUNKS, COLS)),
            dma((DELTA_CHUNKS, ROWS)),
            dma((DELTA_CHUNKS, ROWS)),
            dma((COLS,)),
            dma((COLS,)),
            dma((ROWS,)),
            dma((ROWS,)),
            dma((BACK_CHUNKS, ROWS)),
            dma((BACK_CHUNKS, ROWS)),
            dma((BACK_CHUNKS, COLS)),
            dma((BACK_CHUNKS, COLS)),
            dma((SHARE_CHUNKS, ROWS)),
            dma((SHARE_CHUNKS, ROWS)),
            dma((SHARE_CHUNKS, COLS)),
            dma((SHARE_CHUNKS, COLS)),
        ],
        compiler_params=pltpu.CompilerParams(
            collective_id=0, has_side_effects=True, vmem_limit_bytes=56 << 20
        ),
    )(ids, norm_gain.reshape(1, D), child_delta, parent_hidden, parent_cache, w_query, w_kv)
    tokens = prefix_cache.shape[3]
    context, new_kv = pl.pallas_call(
        prefix_kernel,
        name="prefix_side",
        out_shape=(
            jax.ShapeDtypeStruct((N, HEADS * DH), BF16),
            jax.ShapeDtypeStruct((N, 512), BF16),
        ),
        in_specs=[vmem, vmem, vmem, vmem, hbm],
        out_specs=(vmem, vmem),
        scratch_shapes=[
            pltpu.VMEM((2, tokens, DH), BF16),
            pltpu.VMEM((2, tokens, DH), BF16),
            pltpu.VMEM((N, HEADS * DH), BF16),
            pltpu.VMEM((N, HEADS * DH), F32),
            pltpu.VMEM((2, N, N), F32),
            pltpu.VMEM((N, HEADS * DH), BF16),
            pltpu.VMEM((GROUP * TILE, 1), F32),
            pltpu.VMEM((GROUP * TILE, 1), F32),
            pltpu.VMEM((GROUP * TILE, DH), F32),
            dma((4,)),
        ],
        compiler_params=pltpu.CompilerParams(vmem_limit_bytes=40 << 20),
    )(ids, lens, back, share, prefix_cache.reshape(prefix_cache.shape[1:]))
    return context, new_kv


def solution(mesh):
    return jax.shard_map(
        local,
        mesh=mesh,
        in_specs=(
            P(("row", "col")),
            P(("row", "col")),
            P(("row", "col"), None),
            P(("row", "col"), None),
            P(("row", "col"), None, None, None, None),
            P(("row", "col"), None, None, None, None),
            P(),
            P(),
            P(),
        ),
        out_specs=(P(("row", "col"), None), P(("row", "col"), None)),
        check_vma=False,
    )
```

```python
import math

import jax
import jax.numpy as jnp
from jax import lax
from jax.experimental import pallas as pl
from jax.experimental.pallas import tpu as pltpu
from jax.sharding import PartitionSpec as P

EPSILON = 1e-06
F32 = jnp.float32
BF16 = jnp.bfloat16
I32 = jnp.int32
ROWS = 16
COLS = 8
N = 128
D = 3584
HEADS = 14
GROUP = 7
DH = 128
PARENTS = 32
BLOCK = 128
DELTA_CHUNKS = 2
CHUNK = D // DELTA_CHUNKS
HALF = CHUNK // 2
BACK_CHUNKS = 3
SHARE_CHUNKS = 2
KEYS = 512
EXCLUDED = -1e30
SCORE_SCALE = math.log2(math.e) / math.sqrt(DH)


def iotas(shape):
    return lax.broadcasted_iota(I32, shape, 0), lax.broadcasted_iota(I32, shape, 1)


def one_zero(mask, kind=BF16):
    return jnp.where(mask, 1.0, 0.0).astype(kind)


def to_col(row):
    below, along = iotas((N, N))
    return jnp.sum(jnp.where(below == along, row, 0.0), axis=1, keepdims=True)


def to_row(col):
    below, along = iotas((N, N))
    return jnp.sum(jnp.where(below == along, col, 0.0), axis=0, keepdims=True)


def rank_row(key_row, key_col):
    below, along = iotas((N, N))
    earlier = (key_col == key_row) & (below < along)
    return jnp.sum(jnp.where(earlier, 1.0, 0.0), axis=0, keepdims=True)


def column_order(ids):
    column = ((ids >> 5) & (COLS - 1)).astype(F32)
    return column * 16.0 + rank_row(column, to_col(column))


def dot(a, b):
    return jnp.dot(a, b, preferred_element_type=F32)


def dot_t(a, b):
    return lax.dot_general(a, b, (((1,), (1,)), ((), ())), preferred_element_type=F32)


def pair_rows(left, right):
    width = left.shape[1]
    both = jnp.concatenate(
        [left.reshape(ROWS, 1, 8, width), right.reshape(ROWS, 1, 8, width)], axis=1
    )
    return both.reshape(2 * N, width)


class Exchange:
    def __init__(self, axis, count, me, rows):
        self.axis, self.count, self.me, self.rows = axis, count, me, rows

    def part(self, ref, k):
        return ref.at[pl.ds(pl.multiple_of(k * self.rows, self.rows), self.rows)]

    def copy(self, src, dst, send, recv, k, slot):
        return pltpu.make_async_remote_copy(
            src_ref=self.part(src, k),
            dst_ref=self.part(dst, slot),
            send_sem=send.at[k],
            recv_sem=recv.at[slot],
            device_id={self.axis: k},
            device_id_type=pl.DeviceIdType.MESH,
        )

    def each(self, act):
        def body(k, carry):
            act(lax.rem(self.me + k, self.count))
            return carry

        lax.fori_loop(1, self.count, body, 0)

    def start(self, src, dst, send, recv):
        self.each(lambda k: self.copy(src, dst, send, recv, k, self.me).start())
        own = pl.ds(pl.multiple_of(self.me * self.rows, self.rows), self.rows)
        dst[own, :] = src[own, :]

    def arrived(self, src, dst, send, recv):
        self.each(lambda k: self.copy(src, dst, send, recv, k, k).wait_recv())

    def sent(self, src, dst, send, recv):
        self.each(lambda k: self.copy(src, dst, send, recv, k, self.me).wait_send())


def layer_kernel(
    ids_ref,
    lens_ref,
    gain_ref,
    delta_hbm,
    hidden_hbm,
    blocks_hbm,
    wq_hbm,
    wkv_hbm,
    prefix_hbm,
    context_ref,
    kv_ref,
    delta_v,
    hidden_v,
    blocks_v,
    weight_v,
    out1,
    in1,
    out2,
    in2,
    id_out1,
    id_in1,
    id_out2,
    id_in2,
    wide,
    normed,
    heads_v,
    back1,
    back1_in,
    back2,
    score,
    total,
    prob,
    stat,
    share1,
    share1_in,
    share2,
    back_in,
    share_in,
    prefix_v,
    block_v,
    query_v,
    near_score,
    near_total,
    near_top,
    load_sem,
    d1s,
    d1r,
    d2s,
    d2r,
    i1s,
    i1r,
    i2s,
    i2r,
    b1s,
    b1r,
    b2s,
    b2r,
    s1s,
    s1r,
    s2s,
    s2r,
):
    my_row = lax.axis_index("row")
    my_col = lax.axis_index("col")
    load_delta = pltpu.make_async_copy(delta_hbm, delta_v, load_sem.at[0])
    load_delta.start()

    barrier = pltpu.get_barrier_semaphore()

    def greet_col(k, carry):
        pl.semaphore_signal(
            barrier,
            inc=1,
            device_id={"col": lax.rem(my_col + k, COLS)},
            device_id_type=pl.DeviceIdType.MESH,
        )
        return carry

    def greet_row(k, carry):
        pl.semaphore_signal(
            barrier,
            inc=1,
            device_id={"row": lax.rem(my_row + k, ROWS)},
            device_id_type=pl.DeviceIdType.MESH,
        )
        return carry

    lax.fori_loop(1, COLS, greet_col, 0)
    lax.fori_loop(1, ROWS, greet_row, 0)

    below, along = iotas((N, N))
    ids = ids_ref[...]
    order = column_order(ids)
    pick = order == below.astype(F32)
    sorting = one_zero(pick)
    far_row = (ids >> 8).astype(F32)
    far_local = (ids & (PARENTS - 1)).astype(F32)
    row_sorted = jnp.sum(jnp.where(pick, far_row, 0.0), axis=1, keepdims=True)
    local_sorted = jnp.sum(jnp.where(pick, far_local, 0.0), axis=1, keepdims=True)
    id_out1[...] = jnp.where(along < 64, row_sorted, local_sorted).astype(BF16)

    loads = [
        pltpu.make_async_copy(hidden_hbm, hidden_v, load_sem.at[1]),
        pltpu.make_async_copy(wq_hbm, weight_v.at[:, pl.ds(0, HEADS * DH)], load_sem.at[2]),
        pltpu.make_async_copy(wkv_hbm, weight_v.at[:, pl.ds(HEADS * DH, 512)], load_sem.at[3]),
        pltpu.make_async_copy(blocks_hbm, blocks_v, load_sem.at[4]),
        pltpu.make_async_copy(prefix_hbm, prefix_v, load_sem.at[5]),
    ]
    load_delta.wait()
    for load in loads:
        load.start()
    order_col = to_col(order)
    unsort = one_zero(order_col == along.astype(F32))
    lens_col = to_col(lens_ref[...].astype(F32))
    bias = jnp.where(along.astype(F32) < lens_col, 0.0, EXCLUDED).astype(BF16)
    for h in range(HEADS):
        query_v[h, :, DH:] = bias
    for b in range(prefix_v.shape[2] // BLOCK):
        block_v[b * BLOCK : (b + 1) * BLOCK] = one_zero(along == b)

    by_col = Exchange("col", COLS, my_col, 16)
    by_row = Exchange("row", ROWS, my_row, 16)
    by_row8 = Exchange("row", ROWS, my_row, 8)

    pl.semaphore_wait(barrier, COLS + ROWS - 2)
    by_col.start(id_out1, id_in1, i1s, i1r)
    for c in range(DELTA_CHUNKS):
        out1[c] = dot(sorting, delta_v[:, c * CHUNK : (c + 1) * CHUNK]).astype(BF16)
        by_col.start(out1.at[c], in1.at[c], d1s.at[c], d1r.at[c])

    by_col.arrived(id_out1, id_in1, i1s, i1r)
    arrived_ids = id_in1[...].astype(F32)
    row_col = arrived_ids[:, 0:1]
    row_row = to_row(row_col)
    local_row = to_row(arrived_ids[:, 64:65])
    place = row_row * 8.0 + rank_row(row_row, row_col)
    place_col = to_col(place)
    place_pick = place == below.astype(F32)
    id_out2[...] = jnp.broadcast_to(
        jnp.sum(jnp.where(place_pick, local_row, 0.0), axis=1, keepdims=True), (N, N)
    )
    by_row8.start(id_out2, id_in2, i2s, i2r)

    wide_below, wide_along = iotas((2 * N, 2 * N))
    code_below = ((wide_below >> 4) * 16 + (wide_below & 7) * 2 + ((wide_below >> 3) & 1)).astype(
        F32
    )
    code_along = ((wide_along >> 4) * 16 + (wide_along & 7) * 2 + ((wide_along >> 3) & 1)).astype(
        F32
    )
    code_row = jnp.concatenate([place * 2.0, place * 2.0 + 1.0], axis=1)
    code_col = jnp.concatenate([place_col * 2.0, place_col * 2.0 + 1.0], axis=0)
    forth = one_zero(code_below == code_row)
    turn = one_zero(code_along == code_col)

    for c in range(DELTA_CHUNKS):
        by_col.arrived(out1.at[c], in1.at[c], d1s.at[c], d1r.at[c])
        stacked = jnp.concatenate([in1[c, :, :HALF], in1[c, :, HALF:]], axis=0)
        out2[c] = dot(forth, stacked).astype(BF16)
        by_row.start(out2.at[c], in2.at[c], d2s.at[c], d2r.at[c])

    loads[0].wait()
    by_row8.arrived(id_out2, id_in2, i2s, i2r)
    local_id = id_in2[...]
    owner = one_zero(local_id[:, :PARENTS] == along[:, :PARENTS].astype(F32))
    squares = jnp.zeros((N, 1), F32)
    for c in range(DELTA_CHUNKS):
        by_row.arrived(out2.at[c], in2.at[c], d2s.at[c], d2r.at[c])
        for half in range(2):
            for w in range(HALF // 128):
                at = c * CHUNK + half * HALF + w * 128
                grid = in2[c, :, w * 128 : (w + 1) * 128].astype(F32)
                grid = grid.reshape(ROWS, 2, 8, 128)[:, half].reshape(N, 128)
                value = dot(owner, hidden_v[:, at : at + 128]) + grid
                wide[:, at : at + 128] = value
                squares = squares + jnp.sum(value * value, axis=1, keepdims=True)
    inverse = lax.rsqrt(squares / D + EPSILON)
    for w in range(D // 128):
        at = w * 128
        normed[:, at : at + 128] = (
            wide[:, at : at + 128] * inverse * gain_ref[w : w + 1]
        ).astype(BF16)

    loads[1].wait()
    loads[2].wait()
    for c in range(BACK_CHUNKS):

        def project(t, carry, c=c):
            n = c * 3 + t
            y = dot(normed[...], weight_v[:, pl.ds(pl.multiple_of(n * 256, 256), 256)])
            heads_v[2 * n] = y[:, :128].astype(BF16)
            heads_v[2 * n + 1] = y[:, 128:].astype(BF16)
            back1[c, :, pl.ds(pl.multiple_of(t * 128, 128), 128)] = pair_rows(
                y[:, :128], y[:, 128:]
            ).astype(BF16)
            return carry

        lax.fori_loop(0, 3, project, 0)
        by_row.start(back1.at[c], back1_in.at[c], b1s.at[c], b1r.at[c])

    loads[3].wait()
    score[...] = jnp.zeros_like(score)
    total[...] = jnp.zeros_like(total)

    def masks(k):
        first = (2 * k).astype(F32)
        return one_zero(local_id == first), one_zero(local_id == first + 1.0)

    def score_pair(k, carry):
        mask0, mask1 = masks(k)
        for g in range(2):
            keys = jnp.concatenate([blocks_v[2 * k, 0, g], blocks_v[2 * k + 1, 0, g]], axis=1)
            for h in range(g * GROUP, (g + 1) * GROUP):
                q = heads_v[h]
                score[h] += dot_t(jnp.concatenate([q * mask0, q * mask1], axis=1), keys)
        return carry

    lax.fori_loop(0, PARENTS // 2, score_pair, 0)

    for c in range(BACK_CHUNKS):
        by_row.arrived(back1.at[c], back1_in.at[c], b1s.at[c], b1r.at[c])
        turned = dot(turn, back1_in[c]).astype(BF16)
        for t in range(3):
            back2[c, :, t * 256 : t * 256 + 128] = turned[:N, t * 128 : (t + 1) * 128]
            back2[c, :, t * 256 + 128 : (t + 1) * 256] = turned[N:, t * 128 : (t + 1) * 128]
        by_col.start(back2.at[c], back_in.at[c], b2s.at[c], b2r.at[c])

    for g in range(2):
        stats = jnp.zeros((N, N), F32)
        for h in range(GROUP):
            s = score[g * GROUP + h] * SCORE_SCALE
            top = jnp.max(s, axis=1, keepdims=True)
            e = jnp.exp2(s - top)
            prob[g * GROUP + h] = e.astype(BF16)
            stats = jnp.where(along == h, top, stats)
            stats = jnp.where(along == 8 + h, jnp.sum(e, axis=1, keepdims=True), stats)
        stat[g] = stats

    def value_pair(k, carry):
        mask0, mask1 = masks(k)
        for g in range(2):
            values = jnp.concatenate([blocks_v[2 * k, 1, g], blocks_v[2 * k + 1, 1, g]], axis=0)
            for h in range(g * GROUP, (g + 1) * GROUP):
                p = prob[h]
                total[h] += dot(jnp.concatenate([p * mask0, p * mask1], axis=1), values)
        return carry

    lax.fori_loop(0, PARENTS // 2, value_pair, 0)

    for c in range(SHARE_CHUNKS):
        for b in range(4):
            h = c * 4 + b
            sides = []
            for g in range(2):
                stats = stat[g]
                if h < GROUP:
                    sides.append(total[g * GROUP + h] / stats[:, 8 + h : 9 + h])
                else:
                    high = stats.astype(BF16).astype(F32)
                    rest = stats - high
                    middle = rest.astype(BF16).astype(F32)
                    low = rest - middle
                    sides.append(
                        high + pltpu.roll(middle, shift=16, axis=1) + pltpu.roll(low, shift=32, axis=1)
                    )
            share1[c, :, b * 128 : (b + 1) * 128] = pair_rows(sides[0], sides[1]).astype(BF16)
        by_row.start(share1.at[c], share1_in.at[c], s1s.at[c], s1r.at[c])

    for c in range(BACK_CHUNKS):
        by_col.arrived(back2.at[c], back_in.at[c], b2s.at[c], b2r.at[c])
        own = dot(unsort, back_in[c]).astype(BF16)
        for t in range(3):
            n = c * 3 + t
            if n < GROUP:
                query_v[2 * n, :, :DH] = own[:, t * 256 : t * 256 + 128]
                query_v[2 * n + 1, :, :DH] = own[:, t * 256 + 128 : (t + 1) * 256]
            else:
                kv_ref[:, (n - GROUP) * 256 : (n - GROUP + 1) * 256] = own[
                    :, t * 256 : (t + 1) * 256
                ]
    loads[4].wait()
    spans = [slice(k, k + KEYS) for k in range(0, prefix_v.shape[2], KEYS)]
    ones = jnp.ones((KEYS, DH), BF16)

    def near_scores(h, g, slot):
        q = query_v[h]
        top = jnp.full((N, DH), EXCLUDED, F32)
        for span in spans:
            keys = jnp.concatenate([prefix_v[0, g, span], block_v[span]], axis=1)
            part = dot_t(q, keys)
            near_score[slot, :, span] = part
            for w in range(KEYS // 128):
                top = jnp.maximum(top, part[:, w * 128 : (w + 1) * 128])
        near_top[h] = jnp.broadcast_to(
            jnp.max(top, axis=1, keepdims=True) * SCORE_SCALE, (N, DH)
        )

    def near_values(h, g, slot):
        top = near_top[h][:, :1]
        sums = jnp.zeros((N, 2 * DH), F32)
        for span in spans:
            e = jnp.exp2(near_score[slot, :, span] * SCORE_SCALE - top).astype(BF16)
            sums = sums + dot(e, jnp.concatenate([prefix_v[1, g, span], ones], axis=1))
        near_total[h] = sums

    def head(h, carry):
        later = (h + 1) % HEADS
        near_scores(later, later // GROUP, (h + 1) % 2)
        near_values(h, h // GROUP, h % 2)
        return carry

    near_scores(0, 0, 0)
    lax.fori_loop(0, GROUP, head, 0)

    for c in range(SHARE_CHUNKS):
        by_row.arrived(share1.at[c], share1_in.at[c], s1s.at[c], s1r.at[c])
        turned = dot(turn, share1_in[c]).astype(BF16)
        share2[c, :, :512] = turned[:N]
        share2[c, :, 512:] = turned[N:]
        by_col.start(share2.at[c], share_in.at[c], s2s.at[c], s2r.at[c])

    lax.fori_loop(GROUP, HEADS, head, 0)

    for c in range(SHARE_CHUNKS):
        by_col.arrived(share2.at[c], share_in.at[c], s2s.at[c], s2r.at[c])
    for g in range(2):
        packed = dot(unsort, share_in[1, :, g * 512 + 384 : g * 512 + 512])
        stats = (
            packed
            + pltpu.roll(packed, shift=N - 16, axis=1)
            + pltpu.roll(packed, shift=N - 32, axis=1)
        )
        for h in range(GROUP):
            c, b = h // 4, h % 4
            i = g * GROUP + h
            part = dot(unsort, share_in[c, :, g * 512 + b * 128 : g * 512 + (b + 1) * 128])
            top_far = stats[:, h : h + 1]
            mass_far = stats[:, 8 + h : 9 + h]
            top_near = near_top[i]
            top = jnp.maximum(top_near, top_far)
            near = jnp.exp2(top_near - top)
            far = jnp.exp2(top_far - top) * mass_far
            sums = near_total[i]
            whole = sums[:, DH:] * near + far
            context_ref[:, i * DH : (i + 1) * DH] = (
                (sums[:, :DH] * near + part * far) / whole
            ).astype(BF16)

    by_col.sent(id_out1, id_in1, i1s, i1r)
    by_row8.sent(id_out2, id_in2, i2s, i2r)
    for c in range(DELTA_CHUNKS):
        by_col.sent(out1.at[c], in1.at[c], d1s.at[c], d1r.at[c])
        by_row.sent(out2.at[c], in2.at[c], d2s.at[c], d2r.at[c])
    for c in range(BACK_CHUNKS):
        by_row.sent(back1.at[c], back1_in.at[c], b1s.at[c], b1r.at[c])
        by_col.sent(back2.at[c], back_in.at[c], b2s.at[c], b2r.at[c])
    for c in range(SHARE_CHUNKS):
        by_row.sent(share1.at[c], share1_in.at[c], s1s.at[c], s1r.at[c])
        by_col.sent(share2.at[c], share_in.at[c], s2s.at[c], s2r.at[c])


def local(
    child_parent,
    prefix_len,
    child_delta,
    parent_hidden,
    parent_cache,
    prefix_cache,
    norm_gain,
    w_query,
    w_kv,
):
    vmem = pl.BlockSpec(memory_space=pltpu.VMEM)
    hbm = pl.BlockSpec(memory_space=pl.ANY)
    dma = pltpu.SemaphoreType.DMA
    ids = child_parent.reshape(1, N)
    lens = prefix_len.reshape(1, N)
    tokens = prefix_cache.shape[3]
    back_shape = (BACK_CHUNKS, N, 768)
    share_shape = (SHARE_CHUNKS, N, 1024)
    return pl.pallas_call(
        layer_kernel,
        name="decode_layer",
        out_shape=(
            jax.ShapeDtypeStruct((N, HEADS * DH), BF16),
            jax.ShapeDtypeStruct((N, 512), BF16),
        ),
        in_specs=[vmem, vmem, vmem, hbm, hbm, hbm, hbm, hbm, hbm],
        out_specs=(vmem, vmem),
        scratch_shapes=[
            pltpu.VMEM((N, D), BF16),
            pltpu.VMEM((PARENTS, D), BF16),
            pltpu.VMEM((PARENTS, 2, 2, BLOCK, DH), BF16),
            pltpu.VMEM((D, 2304), BF16),
            pltpu.VMEM((DELTA_CHUNKS, N, CHUNK), BF16),
            pltpu.VMEM((DELTA_CHUNKS, N, CHUNK), BF16),
            pltpu.VMEM((DELTA_CHUNKS, 2 * N, HALF), BF16),
            pltpu.VMEM((DELTA_CHUNKS, 2 * N, HALF), BF16),
            pltpu.VMEM((N, N), BF16),
            pltpu.VMEM((N, N), BF16),
            pltpu.VMEM((N, N), F32),
            pltpu.VMEM((N, N), F32),
            pltpu.VMEM((N, D), F32),
            pltpu.VMEM((N, D), BF16),
            pltpu.VMEM((18, N, 128), BF16),
            pltpu.VMEM((BACK_CHUNKS, 2 * N, 384), BF16),
            pltpu.VMEM((BACK_CHUNKS, 2 * N, 384), BF16),
            pltpu.VMEM(back_shape, BF16),
            pltpu.VMEM((HEADS, N, BLOCK), F32),
            pltpu.VMEM((HEADS, N, DH), F32),
            pltpu.VMEM((HEADS, N, BLOCK), BF16),
            pltpu.VMEM((2, N, N), F32),
            pltpu.VMEM((SHARE_CHUNKS, 2 * N, 512), BF16),
            pltpu.VMEM((SHARE_CHUNKS, 2 * N, 512), BF16),
            pltpu.VMEM(share_shape, BF16),
            pltpu.VMEM(back_shape, BF16),
            pltpu.VMEM(share_shape, BF16),
            pltpu.VMEM((2, 2, tokens, DH), BF16),
            pltpu.VMEM((tokens, BLOCK), BF16),
            pltpu.VMEM((HEADS, N, 2 * DH), BF16),
            pltpu.VMEM((2, N, tokens), F32),
            pltpu.VMEM((HEADS, N, 2 * DH), F32),
            pltpu.VMEM((HEADS, N, DH), F32),
            dma((6,)),
            dma((DELTA_CHUNKS, COLS)),
            dma((DELTA_CHUNKS, COLS)),
            dma((DELTA_CHUNKS, ROWS)),
            dma((DELTA_CHUNKS, ROWS)),
            dma((COLS,)),
            dma((COLS,)),
            dma((ROWS,)),
            dma((ROWS,)),
            dma((BACK_CHUNKS, ROWS)),
            dma((BACK_CHUNKS, ROWS)),
            dma((BACK_CHUNKS, COLS)),
            dma((BACK_CHUNKS, COLS)),
            dma((SHARE_CHUNKS, ROWS)),
            dma((SHARE_CHUNKS, ROWS)),
            dma((SHARE_CHUNKS, COLS)),
            dma((SHARE_CHUNKS, COLS)),
        ],
        compiler_params=pltpu.CompilerParams(
            collective_id=0, has_side_effects=True, vmem_limit_bytes=60 << 20
        ),
    )(
        ids,
        lens,
        norm_gain.reshape(D // 128, 128),
        child_delta,
        parent_hidden,
        parent_cache,
        w_query,
        w_kv,
        prefix_cache.reshape(prefix_cache.shape[1:]),
    )


def solution(mesh):
    return jax.shard_map(
        local,
        mesh=mesh,
        in_specs=(
            P(("row", "col")),
            P(("row", "col")),
            P(("row", "col"), None),
            P(("row", "col"), None),
            P(("row", "col"), None, None, None, None),
            P(("row", "col"), None, None, None, None),
            P(),
            P(),
            P(),
        ),
        out_specs=(P(("row", "col"), None), P(("row", "col"), None)),
        check_vma=False,
    )
```

```python
import math

import jax
import jax.numpy as jnp
from jax import lax
from jax.experimental import pallas as pl
from jax.experimental.pallas import tpu as pltpu
from jax.sharding import PartitionSpec as P

EPSILON = 1e-06
F32 = jnp.float32
BF16 = jnp.bfloat16
I32 = jnp.int32
ROWS = 16
COLS = 8
N = 128
D = 3584
HEADS = 14
GROUP = 7
DH = 128
PARENTS = 32
BLOCK = 128
DELTA_CHUNKS = 2
CHUNK = D // DELTA_CHUNKS
HALF = CHUNK // 2
BACK_CHUNKS = 3
SHARE_CHUNKS = 2
KEYS = 512
TILES = 4
TILE = GROUP * N * 2 // TILES
OCTET = 8
SIDE = N // 2
EXCLUDED = -1e30
SCORE_SCALE = math.log2(math.e) / math.sqrt(DH)


def iotas(shape):
    return lax.broadcasted_iota(I32, shape, 0), lax.broadcasted_iota(I32, shape, 1)


def one_zero(mask, kind=BF16):
    return jnp.where(mask, 1.0, 0.0).astype(kind)


def to_col(row):
    below, along = iotas((N, N))
    return jnp.sum(jnp.where(below == along, row, 0.0), axis=1, keepdims=True)


def to_row(col):
    below, along = iotas((N, N))
    return jnp.sum(jnp.where(below == along, col, 0.0), axis=0, keepdims=True)


def rank_row(key_row, key_col):
    below, along = iotas((N, N))
    earlier = (key_col == key_row) & (below < along)
    return jnp.sum(jnp.where(earlier, 1.0, 0.0), axis=0, keepdims=True)


def column_order(ids):
    column = ((ids >> 5) & (COLS - 1)).astype(F32)
    return column * 16.0 + rank_row(column, to_col(column))


def dot(a, b):
    return jnp.dot(a, b, preferred_element_type=F32)


def dot_t(a, b):
    return lax.dot_general(a, b, (((1,), (1,)), ((), ())), preferred_element_type=F32)


def pair_rows(left, right):
    width = left.shape[1]
    both = jnp.concatenate(
        [left.reshape(ROWS, 1, 8, width), right.reshape(ROWS, 1, 8, width)], axis=1
    )
    return both.reshape(2 * N, width)


class Exchange:
    def __init__(self, axis, count, me, rows):
        self.axis, self.count, self.me, self.rows = axis, count, me, rows

    def part(self, ref, k):
        return ref.at[pl.ds(pl.multiple_of(k * self.rows, self.rows), self.rows)]

    def copy(self, src, dst, send, recv, k, slot):
        return pltpu.make_async_remote_copy(
            src_ref=self.part(src, k),
            dst_ref=self.part(dst, slot),
            send_sem=send.at[k],
            recv_sem=recv.at[slot],
            device_id={self.axis: k},
            device_id_type=pl.DeviceIdType.MESH,
        )

    def each(self, act):
        def body(k, carry):
            act(lax.rem(self.me + k, self.count))
            return carry

        lax.fori_loop(1, self.count, body, 0)

    def start(self, src, dst, send, recv):
        self.each(lambda k: self.copy(src, dst, send, recv, k, self.me).start())
        own = pl.ds(pl.multiple_of(self.me * self.rows, self.rows), self.rows)
        dst[own, :] = src[own, :]

    def arrived(self, src, dst, send, recv):
        self.each(lambda k: self.copy(src, dst, send, recv, k, k).wait_recv())

    def sent(self, src, dst, send, recv):
        self.each(lambda k: self.copy(src, dst, send, recv, k, self.me).wait_send())


def layer_kernel(
    ids_ref,
    lens_ref,
    gain_ref,
    delta_hbm,
    hidden_hbm,
    blocks_hbm,
    wq_hbm,
    wkv_hbm,
    prefix_hbm,
    context_ref,
    kv_ref,
    delta_v,
    hidden_v,
    blocks_v,
    weight_v,
    out1,
    in1,
    out2,
    in2,
    id_out1,
    id_in1,
    id_out2,
    id_in2,
    normed,
    heads_v,
    back1,
    back1_in,
    back2,
    prob,
    stat,
    share1,
    share1_in,
    share2,
    back_in,
    share_in,
    prefix_v,
    block_v,
    query_v,
    near_score,
    near_total,
    near_top,
    load_sem,
    d1s,
    d1r,
    d2s,
    d2r,
    i1s,
    i1r,
    i2s,
    i2r,
    b1s,
    b1r,
    b2s,
    b2r,
    s1s,
    s1r,
    s2s,
    s2r,
):
    my_row = lax.axis_index("row")
    my_col = lax.axis_index("col")
    load_delta = pltpu.make_async_copy(delta_hbm, delta_v, load_sem.at[0])
    load_delta.start()

    barrier = pltpu.get_barrier_semaphore()

    def greet_col(k, carry):
        pl.semaphore_signal(
            barrier,
            inc=1,
            device_id={"col": lax.rem(my_col + k, COLS)},
            device_id_type=pl.DeviceIdType.MESH,
        )
        return carry

    def greet_row(k, carry):
        pl.semaphore_signal(
            barrier,
            inc=1,
            device_id={"row": lax.rem(my_row + k, ROWS)},
            device_id_type=pl.DeviceIdType.MESH,
        )
        return carry

    lax.fori_loop(1, COLS, greet_col, 0)
    lax.fori_loop(1, ROWS, greet_row, 0)

    below, along = iotas((N, N))
    ids = ids_ref[...]
    order = column_order(ids)
    pick = order == below.astype(F32)
    sorting = one_zero(pick)
    far_row = (ids >> 8).astype(F32)
    far_local = (ids & (PARENTS - 1)).astype(F32)
    row_sorted = jnp.sum(jnp.where(pick, far_row, 0.0), axis=1, keepdims=True)
    local_sorted = jnp.sum(jnp.where(pick, far_local, 0.0), axis=1, keepdims=True)
    id_out1[...] = jnp.where(along < 64, row_sorted, local_sorted).astype(BF16)

    loads = [
        pltpu.make_async_copy(hidden_hbm, hidden_v, load_sem.at[1]),
        pltpu.make_async_copy(wq_hbm, weight_v.at[:, pl.ds(0, HEADS * DH)], load_sem.at[2]),
        pltpu.make_async_copy(wkv_hbm, weight_v.at[:, pl.ds(HEADS * DH, 512)], load_sem.at[3]),
        pltpu.make_async_copy(blocks_hbm, blocks_v, load_sem.at[4]),
        pltpu.make_async_copy(prefix_hbm, prefix_v, load_sem.at[5]),
    ]
    load_delta.wait()
    for load in loads:
        load.start()
    order_col = to_col(order)
    unsort = one_zero(order_col == along.astype(F32))
    lens_col = to_col(lens_ref[...].astype(F32))
    bias = jnp.where(along.astype(F32) < lens_col, 0.0, EXCLUDED).astype(BF16)

    def store_query(h, lanes, value):
        at = (h % GROUP) * SIDE
        for side in range(2):
            query_v[(h // GROUP) * 2 + side, at : at + SIDE, lanes] = value[
                side * SIDE : (side + 1) * SIDE
            ]

    for h in range(HEADS):
        store_query(h, slice(DH, 2 * DH), bias)
    for b in range(prefix_v.shape[2] // BLOCK):
        block_v[b * BLOCK : (b + 1) * BLOCK] = one_zero(along == b)

    by_col = Exchange("col", COLS, my_col, 16)
    by_row = Exchange("row", ROWS, my_row, 16)
    by_row8 = Exchange("row", ROWS, my_row, 8)

    wide = near_score.at[0:N, 0:D]
    score = near_score.at[N : 2 * N, 0 : HEADS * DH]
    total = near_score.at[2 * N : 3 * N, 0 : HEADS * DH]
    score[...] = jnp.zeros(score.shape, F32)
    total[...] = jnp.zeros(total.shape, F32)
    pl.semaphore_wait(barrier, COLS + ROWS - 2)
    by_col.start(id_out1, id_in1, i1s, i1r)
    for c in range(DELTA_CHUNKS):
        out1[c] = dot(sorting, delta_v[:, c * CHUNK : (c + 1) * CHUNK]).astype(BF16)
        by_col.start(out1.at[c], in1.at[c], d1s.at[c], d1r.at[c])

    by_col.arrived(id_out1, id_in1, i1s, i1r)
    arrived_ids = id_in1[...].astype(F32)
    row_col = arrived_ids[:, 0:1]
    row_row = to_row(row_col)
    local_row = to_row(arrived_ids[:, 64:65])
    place = row_row * 8.0 + rank_row(row_row, row_col)
    place_col = to_col(place)
    place_pick = place == below.astype(F32)
    id_out2[...] = jnp.broadcast_to(
        jnp.sum(jnp.where(place_pick, local_row, 0.0), axis=1, keepdims=True), (N, N)
    )
    by_row8.start(id_out2, id_in2, i2s, i2r)

    wide_below, wide_along = iotas((2 * N, 2 * N))
    code_below = ((wide_below >> 4) * 16 + (wide_below & 7) * 2 + ((wide_below >> 3) & 1)).astype(
        F32
    )
    code_along = ((wide_along >> 4) * 16 + (wide_along & 7) * 2 + ((wide_along >> 3) & 1)).astype(
        F32
    )
    code_row = jnp.concatenate([place * 2.0, place * 2.0 + 1.0], axis=1)
    code_col = jnp.concatenate([place_col * 2.0, place_col * 2.0 + 1.0], axis=0)
    forth = one_zero(code_below == code_row)
    turn = one_zero(code_along == code_col)

    for c in range(DELTA_CHUNKS):
        by_col.arrived(out1.at[c], in1.at[c], d1s.at[c], d1r.at[c])
        stacked = jnp.concatenate([in1[c, :, :HALF], in1[c, :, HALF:]], axis=0)
        out2[c] = dot(forth, stacked).astype(BF16)
        by_row.start(out2.at[c], in2.at[c], d2s.at[c], d2r.at[c])

    loads[0].wait()
    by_row8.arrived(id_out2, id_in2, i2s, i2r)
    local_id = id_in2[...]
    owner = one_zero(local_id[:, :PARENTS] == along[:, :PARENTS].astype(F32))
    squares = jnp.zeros((N, 1), F32)
    for c in range(DELTA_CHUNKS):
        by_row.arrived(out2.at[c], in2.at[c], d2s.at[c], d2r.at[c])
        for half in range(2):
            for w in range(HALF // 128):
                at = c * CHUNK + half * HALF + w * 128
                grid = in2[c, :, w * 128 : (w + 1) * 128].astype(F32)
                grid = grid.reshape(ROWS, 2, 8, 128)[:, half].reshape(N, 128)
                value = dot(owner, hidden_v[:, at : at + 128]) + grid
                wide[:, at : at + 128] = value
                squares = squares + jnp.sum(value * value, axis=1, keepdims=True)
    inverse = lax.rsqrt(squares / D + EPSILON)
    for w in range(D // 128):
        at = w * 128
        normed[:, at : at + 128] = (
            wide[:, at : at + 128] * inverse * gain_ref[w : w + 1]
        ).astype(BF16)

    loads[1].wait()
    loads[2].wait()
    for c in range(BACK_CHUNKS):

        def project(t, carry, c=c):
            n = c * 3 + t
            y = dot(normed[...], weight_v[:, pl.ds(pl.multiple_of(n * 256, 256), 256)])
            heads_v[2 * n] = y[:, :128].astype(BF16)
            heads_v[2 * n + 1] = y[:, 128:].astype(BF16)
            back1[c, :, pl.ds(pl.multiple_of(t * 128, 128), 128)] = pair_rows(
                y[:, :128], y[:, 128:]
            ).astype(BF16)
            return carry

        lax.fori_loop(0, 3, project, 0)
        by_row.start(back1.at[c], back1_in.at[c], b1s.at[c], b1r.at[c])

    loads[3].wait()

    def pass_back(c):
        by_row.arrived(back1.at[c], back1_in.at[c], b1s.at[c], b1r.at[c])
        turned = dot(turn, back1_in[c]).astype(BF16)
        for t in range(3):
            back2[c, :, t * 256 : t * 256 + 128] = turned[:N, t * 128 : (t + 1) * 128]
            back2[c, :, t * 256 + 128 : (t + 1) * 256] = turned[N:, t * 128 : (t + 1) * 128]
        by_col.start(back2.at[c], back_in.at[c], b2s.at[c], b2r.at[c])

    def masked(source, g, masks):
        return jnp.concatenate(
            [
                jnp.concatenate([source[g * GROUP + h] * mask for mask in masks], axis=1)
                for h in range(GROUP)
            ],
            axis=0,
        )

    def masks_of(k):
        return [one_zero(local_id == (OCTET * k + i).astype(F32)) for i in range(OCTET)]

    def add_heads(target, g, value):
        for h in range(GROUP):
            at = (g * GROUP + h) * DH
            target[:, at : at + DH] += value[h * N : (h + 1) * N]

    def score_octet(k, carry):
        masks = masks_of(k)
        for g in range(2):
            keys = jnp.concatenate([blocks_v[OCTET * k + i, 0, g] for i in range(OCTET)], axis=1)
            add_heads(score, g, dot_t(masked(heads_v, g, masks), keys))
        return carry

    def value_octet(k, carry):
        masks = masks_of(k)
        for g in range(2):
            values = jnp.concatenate([blocks_v[OCTET * k + i, 1, g] for i in range(OCTET)], axis=0)
            add_heads(total, g, dot(masked(prob, g, masks), values))
        return carry

    lax.fori_loop(0, 2, score_octet, 0)
    pass_back(0)
    lax.fori_loop(2, 4, score_octet, 0)
    pass_back(1)

    for g in range(2):
        stats = jnp.zeros((N, N), F32)
        for h in range(GROUP):
            at = (g * GROUP + h) * DH
            s = score[:, at : at + DH] * SCORE_SCALE
            top = jnp.max(s, axis=1, keepdims=True)
            e = jnp.exp2(s - top)
            prob[g * GROUP + h] = e.astype(BF16)
            stats = jnp.where(along == h, top, stats)
            stats = jnp.where(along == 8 + h, jnp.sum(e, axis=1, keepdims=True), stats)
        stat[g] = stats

    lax.fori_loop(0, 2, value_octet, 0)
    pass_back(2)
    lax.fori_loop(2, 4, value_octet, 0)

    for c in range(SHARE_CHUNKS):
        for b in range(4):
            h = c * 4 + b
            sides = []
            for g in range(2):
                stats = stat[g]
                if h < GROUP:
                    at = (g * GROUP + h) * DH
                    sides.append(total[:, at : at + DH] / stats[:, 8 + h : 9 + h])
                else:
                    high = stats.astype(BF16).astype(F32)
                    rest = stats - high
                    middle = rest.astype(BF16).astype(F32)
                    low = rest - middle
                    sides.append(
                        high + pltpu.roll(middle, shift=16, axis=1) + pltpu.roll(low, shift=32, axis=1)
                    )
            share1[c, :, b * 128 : (b + 1) * 128] = pair_rows(sides[0], sides[1]).astype(BF16)
        by_row.start(share1.at[c], share1_in.at[c], s1s.at[c], s1r.at[c])

    for c in range(BACK_CHUNKS):
        by_col.arrived(back2.at[c], back_in.at[c], b2s.at[c], b2r.at[c])
        own = dot(unsort, back_in[c]).astype(BF16)
        for t in range(3):
            n = c * 3 + t
            if n < GROUP:
                for half in range(2):
                    store_query(2 * n + half, slice(0, DH), own[:, t * 256 + half * 128 :][:, :DH])
            else:
                kv_ref[:, (n - GROUP) * 256 : (n - GROUP + 1) * 256] = own[
                    :, t * 256 : (t + 1) * 256
                ]
    loads[4].wait()
    spans = [slice(k, k + KEYS) for k in range(0, prefix_v.shape[2], KEYS)]
    ones = jnp.ones((KEYS, DH), BF16)

    def near_scores(q, g, span, top):
        keys = jnp.concatenate([prefix_v[0, g, span], block_v[span]], axis=1)
        part = dot_t(q, keys)
        near_score[:, span] = part
        for w in range(KEYS // 128):
            top = jnp.maximum(top, part[:, w * 128 : (w + 1) * 128])
        return top

    def near_values(top, g, span, sums):
        e = jnp.exp2(near_score[:, span] * SCORE_SCALE - top).astype(BF16)
        return sums + dot(e, jnp.concatenate([prefix_v[1, g, span], ones], axis=1))

    def keep_top(t, top):
        near_top[t] = jnp.broadcast_to(
            jnp.max(top, axis=1, keepdims=True) * SCORE_SCALE, (TILE, DH)
        )

    def tile(t, carry):
        later = t + 1
        q = query_v[later]
        top = near_top[t][:, :1]
        next_top = jnp.full((TILE, DH), EXCLUDED, F32)
        sums = jnp.zeros((TILE, 2 * DH), F32)
        for span in spans:
            sums = near_values(top, t // 2, span, sums)
            next_top = near_scores(q, later // 2, span, next_top)
        near_total[t] = sums
        keep_top(later, next_top)
        return carry

    first_top = jnp.full((TILE, DH), EXCLUDED, F32)
    for span in spans:
        first_top = near_scores(query_v[0], 0, span, first_top)
    keep_top(0, first_top)
    lax.fori_loop(0, TILES // 2, tile, 0)

    for c in range(SHARE_CHUNKS):
        by_row.arrived(share1.at[c], share1_in.at[c], s1s.at[c], s1r.at[c])
        turned = dot(turn, share1_in[c]).astype(BF16)
        share2[c, :, :512] = turned[:N]
        share2[c, :, 512:] = turned[N:]
        by_col.start(share2.at[c], share_in.at[c], s2s.at[c], s2r.at[c])

    lax.fori_loop(TILES // 2, TILES - 1, tile, 0)
    last_top = near_top[TILES - 1][:, :1]
    last_sums = jnp.zeros((TILE, 2 * DH), F32)
    for span in spans:
        last_sums = near_values(last_top, 1, span, last_sums)
    near_total[TILES - 1] = last_sums

    for c in range(SHARE_CHUNKS):
        by_col.arrived(share2.at[c], share_in.at[c], s2s.at[c], s2r.at[c])
    for g in range(2):
        packed = dot(unsort, share_in[1, :, g * 512 + 384 : g * 512 + 512])
        stats = (
            packed
            + pltpu.roll(packed, shift=N - 16, axis=1)
            + pltpu.roll(packed, shift=N - 32, axis=1)
        )
        for h in range(GROUP):
            c, b = h // 4, h % 4
            i = g * GROUP + h
            part = dot(unsort, share_in[c, :, g * 512 + b * 128 : g * 512 + (b + 1) * 128])
            top_far = stats[:, h : h + 1]
            mass_far = stats[:, 8 + h : 9 + h]
            rows = slice(h * SIDE, (h + 1) * SIDE)
            top_near = jnp.concatenate([near_top[2 * g, rows], near_top[2 * g + 1, rows]], axis=0)
            top = jnp.maximum(top_near, top_far)
            near = jnp.exp2(top_near - top)
            far = jnp.exp2(top_far - top) * mass_far
            sums = jnp.concatenate([near_total[2 * g, rows], near_total[2 * g + 1, rows]], axis=0)
            whole = sums[:, DH:] * near + far
            context_ref[:, i * DH : (i + 1) * DH] = (
                (sums[:, :DH] * near + part * far) / whole
            ).astype(BF16)

    by_col.sent(id_out1, id_in1, i1s, i1r)
    by_row8.sent(id_out2, id_in2, i2s, i2r)
    for c in range(DELTA_CHUNKS):
        by_col.sent(out1.at[c], in1.at[c], d1s.at[c], d1r.at[c])
        by_row.sent(out2.at[c], in2.at[c], d2s.at[c], d2r.at[c])
    for c in range(BACK_CHUNKS):
        by_row.sent(back1.at[c], back1_in.at[c], b1s.at[c], b1r.at[c])
        by_col.sent(back2.at[c], back_in.at[c], b2s.at[c], b2r.at[c])
    for c in range(SHARE_CHUNKS):
        by_row.sent(share1.at[c], share1_in.at[c], s1s.at[c], s1r.at[c])
        by_col.sent(share2.at[c], share_in.at[c], s2s.at[c], s2r.at[c])


def local(
    child_parent,
    prefix_len,
    child_delta,
    parent_hidden,
    parent_cache,
    prefix_cache,
    norm_gain,
    w_query,
    w_kv,
):
    vmem = pl.BlockSpec(memory_space=pltpu.VMEM)
    hbm = pl.BlockSpec(memory_space=pl.ANY)
    dma = pltpu.SemaphoreType.DMA
    ids = child_parent.reshape(1, N)
    lens = prefix_len.reshape(1, N)
    tokens = prefix_cache.shape[3]
    back_shape = (BACK_CHUNKS, N, 768)
    share_shape = (SHARE_CHUNKS, N, 1024)
    return pl.pallas_call(
        layer_kernel,
        name="decode_layer",
        out_shape=(
            jax.ShapeDtypeStruct((N, HEADS * DH), BF16),
            jax.ShapeDtypeStruct((N, 512), BF16),
        ),
        in_specs=[vmem, vmem, vmem, hbm, hbm, hbm, hbm, hbm, hbm],
        out_specs=(vmem, vmem),
        scratch_shapes=[
            pltpu.VMEM((N, D), BF16),
            pltpu.VMEM((PARENTS, D), BF16),
            pltpu.VMEM((PARENTS, 2, 2, BLOCK, DH), BF16),
            pltpu.VMEM((D, 2304), BF16),
            pltpu.VMEM((DELTA_CHUNKS, N, CHUNK), BF16),
            pltpu.VMEM((DELTA_CHUNKS, N, CHUNK), BF16),
            pltpu.VMEM((DELTA_CHUNKS, 2 * N, HALF), BF16),
            pltpu.VMEM((DELTA_CHUNKS, 2 * N, HALF), BF16),
            pltpu.VMEM((N, N), BF16),
            pltpu.VMEM((N, N), BF16),
            pltpu.VMEM((N, N), F32),
            pltpu.VMEM((N, N), F32),
            pltpu.VMEM((N, D), BF16),
            pltpu.VMEM((18, N, 128), BF16),
            pltpu.VMEM((BACK_CHUNKS, 2 * N, 384), BF16),
            pltpu.VMEM((BACK_CHUNKS, 2 * N, 384), BF16),
            pltpu.VMEM(back_shape, BF16),
            pltpu.VMEM((HEADS, N, BLOCK), BF16),
            pltpu.VMEM((2, N, N), F32),
            pltpu.VMEM((SHARE_CHUNKS, 2 * N, 512), BF16),
            pltpu.VMEM((SHARE_CHUNKS, 2 * N, 512), BF16),
            pltpu.VMEM(share_shape, BF16),
            pltpu.VMEM(back_shape, BF16),
            pltpu.VMEM(share_shape, BF16),
            pltpu.VMEM((2, 2, tokens, DH), BF16),
            pltpu.VMEM((tokens, BLOCK), BF16),
            pltpu.VMEM((TILES, TILE, 2 * DH), BF16),
            pltpu.VMEM((TILE, tokens), F32),
            pltpu.VMEM((TILES, TILE, 2 * DH), F32),
            pltpu.VMEM((TILES, TILE, DH), F32),
            dma((6,)),
            dma((DELTA_CHUNKS, COLS)),
            dma((DELTA_CHUNKS, COLS)),
            dma((DELTA_CHUNKS, ROWS)),
            dma((DELTA_CHUNKS, ROWS)),
            dma((COLS,)),
            dma((COLS,)),
            dma((ROWS,)),
            dma((ROWS,)),
            dma((BACK_CHUNKS, ROWS)),
            dma((BACK_CHUNKS, ROWS)),
            dma((BACK_CHUNKS, COLS)),
            dma((BACK_CHUNKS, COLS)),
            dma((SHARE_CHUNKS, ROWS)),
            dma((SHARE_CHUNKS, ROWS)),
            dma((SHARE_CHUNKS, COLS)),
            dma((SHARE_CHUNKS, COLS)),
        ],
        compiler_params=pltpu.CompilerParams(
            collective_id=0, has_side_effects=True, vmem_limit_bytes=60 << 20
        ),
    )(
        ids,
        lens,
        norm_gain.reshape(D // 128, 128),
        child_delta,
        parent_hidden,
        parent_cache,
        w_query,
        w_kv,
        prefix_cache.reshape(prefix_cache.shape[1:]),
    )


def solution(mesh):
    return jax.shard_map(
        local,
        mesh=mesh,
        in_specs=(
            P(("row", "col")),
            P(("row", "col")),
            P(("row", "col"), None),
            P(("row", "col"), None),
            P(("row", "col"), None, None, None, None),
            P(("row", "col"), None, None, None, None),
            P(),
            P(),
            P(),
        ),
        out_specs=(P(("row", "col"), None), P(("row", "col"), None)),
        check_vma=False,
    )
```

```python
import math

import jax
import jax.numpy as jnp
from jax import lax
from jax.experimental import pallas as pl
from jax.experimental.pallas import tpu as pltpu
from jax.sharding import PartitionSpec as P

EPSILON = 1e-06
F32 = jnp.float32
BF16 = jnp.bfloat16
I32 = jnp.int32
ROWS = 16
COLS = 8
N = 128
D = 3584
HEADS = 14
GROUP = 7
DH = 128
PARENTS = 32
BLOCK = 128
DELTA_HALVES = (512, 512, 384, 384)
DELTA_STARTS = (0, 1024, 2048, 2816)
DELTA_CHUNKS = 4
BACK_TILES = (4, 3, 2)
BACK_STARTS = (0, 4, 7)
BACK_CHUNKS = 3
SHARE_CHUNKS = 2
KEYS = 512
TILES = 4
TILE = GROUP * N * 2 // TILES
PAIRS = 8
SIDE = N // 2
EXCLUDED = -1e30
SCORE_SCALE = math.log2(math.e) / math.sqrt(DH)


def iotas(shape):
    return lax.broadcasted_iota(I32, shape, 0), lax.broadcasted_iota(I32, shape, 1)


def one_zero(mask, kind=BF16):
    return jnp.where(mask, 1.0, 0.0).astype(kind)


def to_col(row):
    below, along = iotas((N, N))
    return jnp.sum(jnp.where(below == along, row, 0.0), axis=1, keepdims=True)


def to_row(col):
    below, along = iotas((N, N))
    return jnp.sum(jnp.where(below == along, col, 0.0), axis=0, keepdims=True)


def rank_row(key_row, key_col):
    below, along = iotas((N, N))
    earlier = (key_col == key_row) & (below < along)
    return jnp.sum(jnp.where(earlier, 1.0, 0.0), axis=0, keepdims=True)


def column_order(ids):
    column = ((ids >> 5) & (COLS - 1)).astype(F32)
    return column * 16.0 + rank_row(column, to_col(column))


def dot(a, b):
    return jnp.dot(a, b, preferred_element_type=F32)


def dot_t(a, b):
    return lax.dot_general(a, b, (((1,), (1,)), ((), ())), preferred_element_type=F32)


def pair_rows(left, right):
    width = left.shape[1]
    both = jnp.concatenate(
        [left.reshape(ROWS, 1, 8, width), right.reshape(ROWS, 1, 8, width)], axis=1
    )
    return both.reshape(2 * N, width)


class Exchange:
    def __init__(self, axis, count, me, rows):
        self.axis, self.count, self.me, self.rows = axis, count, me, rows

    def part(self, ref, k):
        return ref.at[pl.ds(pl.multiple_of(k * self.rows, self.rows), self.rows)]

    def copy(self, src, dst, send, recv, k, slot):
        return pltpu.make_async_remote_copy(
            src_ref=self.part(src, k),
            dst_ref=self.part(dst, slot),
            send_sem=send.at[k],
            recv_sem=recv.at[slot],
            device_id={self.axis: k},
            device_id_type=pl.DeviceIdType.MESH,
        )

    def each(self, act):
        def body(k, carry):
            act(lax.rem(self.me + k, self.count))
            return carry

        lax.fori_loop(1, self.count, body, 0)

    def start(self, src, dst, send, recv):
        self.each(lambda k: self.copy(src, dst, send, recv, k, self.me).start())
        own = pl.ds(pl.multiple_of(self.me * self.rows, self.rows), self.rows)
        dst[own, :] = src[own, :]

    def arrived(self, src, dst, send, recv):
        self.each(lambda k: self.copy(src, dst, send, recv, k, k).wait_recv())

    def sent(self, src, dst, send, recv):
        self.each(lambda k: self.copy(src, dst, send, recv, k, self.me).wait_send())


def layer_kernel(
    ids_ref,
    lens_ref,
    gain_ref,
    delta_hbm,
    hidden_hbm,
    blocks_hbm,
    wq_hbm,
    wkv_hbm,
    prefix_hbm,
    context_ref,
    kv_ref,
    delta_v,
    hidden_v,
    blocks_v,
    weight_v,
    out1,
    in1,
    out2,
    in2,
    id_out1,
    id_in1,
    id_out2,
    id_in2,
    normed,
    heads_v,
    back1,
    back1_in,
    back2,
    prob,
    stat,
    share1,
    share1_in,
    share2,
    back_in,
    share_in,
    prefix_v,
    block_v,
    query_v,
    near_score,
    near_total,
    near_top,
    kv_v,
    context_v,
    save_sem,
    load_sem,
    d1s,
    d1r,
    d2s,
    d2r,
    i1s,
    i1r,
    i2s,
    i2r,
    b1s,
    b1r,
    b2s,
    b2r,
    s1s,
    s1r,
    s2s,
    s2r,
):
    my_row = lax.axis_index("row")
    my_col = lax.axis_index("col")
    load_delta = pltpu.make_async_copy(delta_hbm, delta_v, load_sem.at[0])
    load_delta.start()

    barrier = pltpu.get_barrier_semaphore()

    def greet_col(k, carry):
        pl.semaphore_signal(
            barrier,
            inc=1,
            device_id={"col": lax.rem(my_col + k, COLS)},
            device_id_type=pl.DeviceIdType.MESH,
        )
        return carry

    def greet_row(k, carry):
        pl.semaphore_signal(
            barrier,
            inc=1,
            device_id={"row": lax.rem(my_row + k, ROWS)},
            device_id_type=pl.DeviceIdType.MESH,
        )
        return carry

    lax.fori_loop(1, COLS, greet_col, 0)
    lax.fori_loop(1, ROWS, greet_row, 0)

    below, along = iotas((N, N))
    ids = ids_ref[...]
    order = column_order(ids)
    pick = order == below.astype(F32)
    sorting = one_zero(pick)
    far_row = (ids >> 8).astype(F32)
    far_local = (ids & (PARENTS - 1)).astype(F32)
    row_sorted = jnp.sum(jnp.where(pick, far_row, 0.0), axis=1, keepdims=True)
    local_sorted = jnp.sum(jnp.where(pick, far_local, 0.0), axis=1, keepdims=True)
    id_out1[...] = jnp.where(along < 64, row_sorted, local_sorted).astype(BF16)

    loads = [
        pltpu.make_async_copy(hidden_hbm, hidden_v, load_sem.at[1]),
        pltpu.make_async_copy(wq_hbm, weight_v.at[:, pl.ds(0, HEADS * DH)], load_sem.at[2]),
        pltpu.make_async_copy(wkv_hbm, weight_v.at[:, pl.ds(HEADS * DH, 512)], load_sem.at[3]),
        pltpu.make_async_copy(blocks_hbm, blocks_v, load_sem.at[4]),
        pltpu.make_async_copy(prefix_hbm, prefix_v, load_sem.at[5]),
    ]
    load_delta.wait()
    for load in loads:
        load.start()
    order_col = to_col(order)
    unsort = one_zero(order_col == along.astype(F32))
    lens_col = to_col(lens_ref[...].astype(F32))
    bias = jnp.where(along.astype(F32) < lens_col, 0.0, EXCLUDED).astype(BF16)

    by_col = Exchange("col", COLS, my_col, 16)
    by_row = Exchange("row", ROWS, my_row, 16)
    by_row8 = Exchange("row", ROWS, my_row, 8)

    pl.semaphore_wait(barrier, COLS + ROWS - 2)
    by_col.start(id_out1, id_in1, i1s, i1r)
    for c in range(DELTA_CHUNKS):
        first = DELTA_STARTS[c]
        out1[c][...] = dot(sorting, delta_v[:, first : first + 2 * DELTA_HALVES[c]]).astype(BF16)
        by_col.start(out1[c], in1[c], d1s.at[c], d1r.at[c])

    wide = near_score.at[0:N, 0:D]
    score = near_score.at[N : 2 * N, 0 : 2 * HEADS * DH]
    total = near_score.at[2 * N : 3 * N, 0 : 2 * HEADS * DH]
    score[...] = jnp.zeros(score.shape, F32)
    total[...] = jnp.zeros(total.shape, F32)
    def store_query(h, lanes, value):
        at = (h % GROUP) * SIDE
        for side in range(2):
            query_v[(h // GROUP) * 2 + side, at : at + SIDE, lanes] = value[
                side * SIDE : (side + 1) * SIDE
            ]

    for h in range(HEADS):
        store_query(h, slice(DH, 2 * DH), bias)
    for b in range(prefix_v.shape[2] // BLOCK):
        block_v[b * BLOCK : (b + 1) * BLOCK] = one_zero(along == b)

    by_col.arrived(id_out1, id_in1, i1s, i1r)
    arrived_ids = id_in1[...].astype(F32)
    row_col = arrived_ids[:, 0:1]
    row_row = to_row(row_col)
    local_row = to_row(arrived_ids[:, 64:65])
    place = row_row * 8.0 + rank_row(row_row, row_col)
    place_col = to_col(place)
    place_pick = place == below.astype(F32)
    id_out2[...] = jnp.broadcast_to(
        jnp.sum(jnp.where(place_pick, local_row, 0.0), axis=1, keepdims=True), (N, N)
    )
    by_row8.start(id_out2, id_in2, i2s, i2r)

    wide_below, wide_along = iotas((2 * N, 2 * N))
    code_below = ((wide_below >> 4) * 16 + (wide_below & 7) * 2 + ((wide_below >> 3) & 1)).astype(
        F32
    )
    code_along = ((wide_along >> 4) * 16 + (wide_along & 7) * 2 + ((wide_along >> 3) & 1)).astype(
        F32
    )
    code_row = jnp.concatenate([place * 2.0, place * 2.0 + 1.0], axis=1)
    code_col = jnp.concatenate([place_col * 2.0, place_col * 2.0 + 1.0], axis=0)
    forth = one_zero(code_below == code_row)
    turn = one_zero(code_along == code_col)

    for c in range(DELTA_CHUNKS):
        by_col.arrived(out1[c], in1[c], d1s.at[c], d1r.at[c])
        width = DELTA_HALVES[c]
        stacked = jnp.concatenate([in1[c][:, :width], in1[c][:, width:]], axis=0)
        out2[c][...] = dot(forth, stacked).astype(BF16)
        by_row.start(out2[c], in2[c], d2s.at[c], d2r.at[c])

    loads[0].wait()
    by_row8.arrived(id_out2, id_in2, i2s, i2r)
    local_id = id_in2[...]
    owner = one_zero(local_id[:, :PARENTS] == along[:, :PARENTS].astype(F32))
    squares = jnp.zeros((N, 1), F32)
    for c in range(DELTA_CHUNKS):
        by_row.arrived(out2[c], in2[c], d2s.at[c], d2r.at[c])
        for half in range(2):
            for w in range(DELTA_HALVES[c] // 128):
                at = DELTA_STARTS[c] + half * DELTA_HALVES[c] + w * 128
                grid = in2[c][:, w * 128 : (w + 1) * 128].astype(F32)
                grid = grid.reshape(ROWS, 2, 8, 128)[:, half].reshape(N, 128)
                value = dot(owner, hidden_v[:, at : at + 128]) + grid
                wide[:, at : at + 128] = value
                squares = squares + jnp.sum(value * value, axis=1, keepdims=True)
    inverse = lax.rsqrt(squares / D + EPSILON)
    for w in range(D // 128):
        at = w * 128
        normed[:, at : at + 128] = (
            wide[:, at : at + 128] * inverse * gain_ref[w : w + 1]
        ).astype(BF16)

    loads[1].wait()
    loads[2].wait()
    for c in range(BACK_CHUNKS):

        def project(t, carry, c=c):
            n = BACK_STARTS[c] + t
            y = dot(normed[...], weight_v[:, pl.ds(pl.multiple_of(n * 256, 256), 256)])
            heads_v[2 * n] = y[:, :128].astype(BF16)
            heads_v[2 * n + 1] = y[:, 128:].astype(BF16)
            back1[c][:, pl.ds(pl.multiple_of(t * 128, 128), 128)] = pair_rows(
                y[:, :128], y[:, 128:]
            ).astype(BF16)
            return carry

        lax.fori_loop(0, BACK_TILES[c], project, 0)
        by_row.start(back1[c], back1_in[c], b1s.at[c], b1r.at[c])

    loads[3].wait()

    def pass_back(c):
        by_row.arrived(back1[c], back1_in[c], b1s.at[c], b1r.at[c])
        turned = dot(turn, back1_in[c][...]).astype(BF16)
        for t in range(BACK_TILES[c]):
            back2[c][:, t * 256 : t * 256 + 128] = turned[:N, t * 128 : (t + 1) * 128]
            back2[c][:, t * 256 + 128 : (t + 1) * 256] = turned[N:, t * 128 : (t + 1) * 128]
        by_col.start(back2[c], back_in[c], b2s.at[c], b2r.at[c])

    def masked(source, g, masks):
        return jnp.concatenate(
            [
                jnp.concatenate([source[g * GROUP + h] * mask for mask in masks], axis=1)
                for h in range(GROUP)
            ],
            axis=0,
        )

    pair_id = jnp.floor(local_id * 0.5)
    second = local_id != pair_id * 2.0

    def masks_of(k):
        return [one_zero(pair_id == (PAIRS * k + i).astype(F32)) for i in range(PAIRS)]

    def add_heads(target, g, value):
        for h in range(GROUP):
            at = (g * GROUP + h) * 2 * DH
            target[:, at : at + 2 * DH] += value[h * N : (h + 1) * N]

    def blocks_of(k, kind, g, side, axis):
        return jnp.concatenate(
            [blocks_v[2 * (PAIRS * k + i) + side, kind, g] for i in range(PAIRS)], axis=axis
        )

    def score_step(k, carry):
        masks = masks_of(k)
        for g in range(2):
            keys = jnp.concatenate([blocks_of(k, 0, g, side, 1) for side in range(2)], axis=0)
            add_heads(score, g, dot_t(masked(heads_v, g, masks), keys))
        return carry

    def value_step(k, carry):
        masks = masks_of(k)
        for g in range(2):
            values = jnp.concatenate([blocks_of(k, 1, g, side, 0) for side in range(2)], axis=1)
            add_heads(total, g, dot(masked(prob, g, masks), values))
        return carry

    def side_of(source, i):
        at = i * 2 * DH
        return jnp.where(second, source[:, at + DH : at + 2 * DH], source[:, at : at + DH])

    lax.fori_loop(0, 1, score_step, 0)
    pass_back(0)
    lax.fori_loop(1, 2, score_step, 0)
    pass_back(1)

    for g in range(2):
        stats = jnp.zeros((N, N), F32)
        for h in range(GROUP):
            s = side_of(score, g * GROUP + h) * SCORE_SCALE
            top = jnp.max(s, axis=1, keepdims=True)
            e = jnp.exp2(s - top)
            prob[g * GROUP + h] = e.astype(BF16)
            stats = jnp.where(along == h, top, stats)
            stats = jnp.where(along == 8 + h, jnp.sum(e, axis=1, keepdims=True), stats)
        stat[g] = stats

    lax.fori_loop(0, 1, value_step, 0)
    pass_back(2)
    lax.fori_loop(1, 2, value_step, 0)

    for c in range(SHARE_CHUNKS):
        for b in range(4):
            h = c * 4 + b
            sides = []
            for g in range(2):
                stats = stat[g]
                if h < GROUP:
                    sides.append(side_of(total, g * GROUP + h) / stats[:, 8 + h : 9 + h])
                else:
                    high = stats.astype(BF16).astype(F32)
                    rest = stats - high
                    middle = rest.astype(BF16).astype(F32)
                    low = rest - middle
                    sides.append(
                        high + pltpu.roll(middle, shift=16, axis=1) + pltpu.roll(low, shift=32, axis=1)
                    )
            share1[c, :, b * 128 : (b + 1) * 128] = pair_rows(sides[0], sides[1]).astype(BF16)
        by_row.start(share1.at[c], share1_in.at[c], s1s.at[c], s1r.at[c])

    def take_back(c):
        by_col.arrived(back2[c], back_in[c], b2s.at[c], b2r.at[c])
        own = dot(unsort, back_in[c][...]).astype(BF16)
        for t in range(BACK_TILES[c]):
            n = BACK_STARTS[c] + t
            if n < GROUP:
                for half in range(2):
                    store_query(2 * n + half, slice(0, DH), own[:, t * 256 + half * 128 :][:, :DH])
            else:
                kv_v[:, (n - GROUP) * 256 : (n - GROUP + 1) * 256] = own[
                    :, t * 256 : (t + 1) * 256
                ]

    take_back(0)
    loads[4].wait()
    spans = [slice(k, k + KEYS) for k in range(0, prefix_v.shape[2], KEYS)]
    ones = jnp.ones((KEYS, DH), BF16)

    def near_scores(q, g, span, top):
        keys = jnp.concatenate([prefix_v[0, g, span], block_v[span]], axis=1)
        part = dot_t(q, keys)
        near_score[:, span] = part
        for w in range(KEYS // 128):
            top = jnp.maximum(top, part[:, w * 128 : (w + 1) * 128])
        return top

    def near_values(top, g, span, sums):
        e = jnp.exp2(near_score[:, span] * SCORE_SCALE - top).astype(BF16)
        return sums + dot(e, jnp.concatenate([prefix_v[1, g, span], ones], axis=1))

    def keep_top(t, top):
        near_top[t] = jnp.broadcast_to(
            jnp.max(top, axis=1, keepdims=True) * SCORE_SCALE, (TILE, DH)
        )

    def tile(t, carry):
        later = t + 1
        q = query_v[later]
        top = near_top[t][:, :1]
        next_top = jnp.full((TILE, DH), EXCLUDED, F32)
        sums = jnp.zeros((TILE, 2 * DH), F32)
        for span in spans:
            sums = near_values(top, t // 2, span, sums)
            next_top = near_scores(q, later // 2, span, next_top)
        near_total[t] = sums
        keep_top(later, next_top)
        return carry

    first_top = jnp.full((TILE, DH), EXCLUDED, F32)
    for span in spans:
        first_top = near_scores(query_v[0], 0, span, first_top)
    keep_top(0, first_top)
    lax.fori_loop(0, 1, tile, 0)
    take_back(1)

    for c in range(SHARE_CHUNKS):
        by_row.arrived(share1.at[c], share1_in.at[c], s1s.at[c], s1r.at[c])
        turned = dot(turn, share1_in[c]).astype(BF16)
        share2[c, :, :512] = turned[:N]
        share2[c, :, 512:] = turned[N:]
        by_col.start(share2.at[c], share_in.at[c], s2s.at[c], s2r.at[c])

    lax.fori_loop(1, TILES - 1, tile, 0)
    take_back(2)
    save_kv = pltpu.make_async_copy(kv_v, kv_ref, save_sem.at[2])
    save_kv.start()
    last_top = near_top[TILES - 1][:, :1]
    last_sums = jnp.zeros((TILE, 2 * DH), F32)
    for span in spans:
        last_sums = near_values(last_top, 1, span, last_sums)
    near_total[TILES - 1] = last_sums

    for c in range(SHARE_CHUNKS):
        by_col.arrived(share2.at[c], share_in.at[c], s2s.at[c], s2r.at[c])
    saves = [save_kv]
    for g in range(2):
        packed = dot(unsort, share_in[1, :, g * 512 + 384 : g * 512 + 512])
        stats = (
            packed
            + pltpu.roll(packed, shift=N - 16, axis=1)
            + pltpu.roll(packed, shift=N - 32, axis=1)
        )
        for h in range(GROUP):
            c, b = h // 4, h % 4
            i = g * GROUP + h
            part = dot(unsort, share_in[c, :, g * 512 + b * 128 : g * 512 + (b + 1) * 128])
            top_far = stats[:, h : h + 1]
            mass_far = stats[:, 8 + h : 9 + h]
            rows = slice(h * SIDE, (h + 1) * SIDE)
            top_near = jnp.concatenate([near_top[2 * g, rows], near_top[2 * g + 1, rows]], axis=0)
            top = jnp.maximum(top_near, top_far)
            near = jnp.exp2(top_near - top)
            far = jnp.exp2(top_far - top) * mass_far
            sums = jnp.concatenate([near_total[2 * g, rows], near_total[2 * g + 1, rows]], axis=0)
            whole = sums[:, DH:] * near + far
            context_v[:, i * DH : (i + 1) * DH] = (
                (sums[:, :DH] * near + part * far) / whole
            ).astype(BF16)

        lanes = pl.ds(g * GROUP * DH, GROUP * DH)
        save = pltpu.make_async_copy(
            context_v.at[:, lanes], context_ref.at[:, lanes], save_sem.at[g]
        )
        save.start()
        saves.append(save)

    by_col.sent(id_out1, id_in1, i1s, i1r)
    by_row8.sent(id_out2, id_in2, i2s, i2r)
    for c in range(DELTA_CHUNKS):
        by_col.sent(out1[c], in1[c], d1s.at[c], d1r.at[c])
        by_row.sent(out2[c], in2[c], d2s.at[c], d2r.at[c])
    for c in range(BACK_CHUNKS):
        by_row.sent(back1[c], back1_in[c], b1s.at[c], b1r.at[c])
        by_col.sent(back2[c], back_in[c], b2s.at[c], b2r.at[c])
    for c in range(SHARE_CHUNKS):
        by_row.sent(share1.at[c], share1_in.at[c], s1s.at[c], s1r.at[c])
        by_col.sent(share2.at[c], share_in.at[c], s2s.at[c], s2r.at[c])
    for save in saves:
        save.wait()


def result_kernel(context_in, kv_in, context_ref, kv_ref, sem):
    copies = [
        pltpu.make_async_copy(context_in, context_ref, sem.at[0]),
        pltpu.make_async_copy(kv_in, kv_ref, sem.at[1]),
    ]
    for copy in copies:
        copy.start()
    for copy in copies:
        copy.wait()


def local(
    child_parent,
    prefix_len,
    child_delta,
    parent_hidden,
    parent_cache,
    prefix_cache,
    norm_gain,
    w_query,
    w_kv,
):
    vmem = pl.BlockSpec(memory_space=pltpu.VMEM)
    hbm = pl.BlockSpec(memory_space=pl.ANY)
    dma = pltpu.SemaphoreType.DMA
    ids = child_parent.reshape(1, N)
    lens = prefix_len.reshape(1, N)
    tokens = prefix_cache.shape[3]
    share_shape = (SHARE_CHUNKS, N, 1024)
    results = (
        jax.ShapeDtypeStruct((N, HEADS * DH), BF16),
        jax.ShapeDtypeStruct((N, 512), BF16),
    )
    context, new_kv = pl.pallas_call(
        layer_kernel,
        name="decode_layer",
        out_shape=results,
        in_specs=[vmem, vmem, vmem, hbm, hbm, hbm, hbm, hbm, hbm],
        out_specs=(hbm, hbm),
        scratch_shapes=[
            pltpu.VMEM((N, D), BF16),
            pltpu.VMEM((PARENTS, D), BF16),
            pltpu.VMEM((PARENTS, 2, 2, BLOCK, DH), BF16),
            pltpu.VMEM((D, 2304), BF16),
            [pltpu.VMEM((N, 2 * half), BF16) for half in DELTA_HALVES],
            [pltpu.VMEM((N, 2 * half), BF16) for half in DELTA_HALVES],
            [pltpu.VMEM((2 * N, half), BF16) for half in DELTA_HALVES],
            [pltpu.VMEM((2 * N, half), BF16) for half in DELTA_HALVES],
            pltpu.VMEM((N, N), BF16),
            pltpu.VMEM((N, N), BF16),
            pltpu.VMEM((N, N), F32),
            pltpu.VMEM((N, N), F32),
            pltpu.VMEM((N, D), BF16),
            pltpu.VMEM((18, N, 128), BF16),
            [pltpu.VMEM((2 * N, tiles * 128), BF16) for tiles in BACK_TILES],
            [pltpu.VMEM((2 * N, tiles * 128), BF16) for tiles in BACK_TILES],
            [pltpu.VMEM((N, tiles * 256), BF16) for tiles in BACK_TILES],
            pltpu.VMEM((HEADS, N, BLOCK), BF16),
            pltpu.VMEM((2, N, N), F32),
            pltpu.VMEM((SHARE_CHUNKS, 2 * N, 512), BF16),
            pltpu.VMEM((SHARE_CHUNKS, 2 * N, 512), BF16),
            pltpu.VMEM(share_shape, BF16),
            [pltpu.VMEM((N, tiles * 256), BF16) for tiles in BACK_TILES],
            pltpu.VMEM(share_shape, BF16),
            pltpu.VMEM((2, 2, tokens, DH), BF16),
            pltpu.VMEM((tokens, BLOCK), BF16),
            pltpu.VMEM((TILES, TILE, 2 * DH), BF16),
            pltpu.VMEM((TILE, tokens), F32),
            pltpu.VMEM((TILES, TILE, 2 * DH), F32),
            pltpu.VMEM((TILES, TILE, DH), F32),
            pltpu.VMEM((N, 512), BF16),
            pltpu.VMEM((N, HEADS * DH), BF16),
            dma((3,)),
            dma((6,)),
            dma((DELTA_CHUNKS, COLS)),
            dma((DELTA_CHUNKS, COLS)),
            dma((DELTA_CHUNKS, ROWS)),
            dma((DELTA_CHUNKS, ROWS)),
            dma((COLS,)),
            dma((COLS,)),
            dma((ROWS,)),
            dma((ROWS,)),
            dma((BACK_CHUNKS, ROWS)),
            dma((BACK_CHUNKS, ROWS)),
            dma((BACK_CHUNKS, COLS)),
            dma((BACK_CHUNKS, COLS)),
            dma((SHARE_CHUNKS, ROWS)),
            dma((SHARE_CHUNKS, ROWS)),
            dma((SHARE_CHUNKS, COLS)),
            dma((SHARE_CHUNKS, COLS)),
        ],
        compiler_params=pltpu.CompilerParams(
            collective_id=0, has_side_effects=True, vmem_limit_bytes=60 << 20
        ),
    )(
        ids,
        lens,
        norm_gain.reshape(D // 128, 128),
        child_delta,
        parent_hidden,
        parent_cache,
        w_query,
        w_kv,
        prefix_cache.reshape(prefix_cache.shape[1:]),
    )
    return pl.pallas_call(
        result_kernel,
        name="results",
        out_shape=results,
        in_specs=[hbm, hbm],
        out_specs=(hbm, hbm),
        scratch_shapes=[dma((2,))],
        compiler_params=pltpu.CompilerParams(vmem_limit_bytes=60 << 20),
    )(context, new_kv)


def solution(mesh):
    return jax.shard_map(
        local,
        mesh=mesh,
        in_specs=(
            P(("row", "col")),
            P(("row", "col")),
            P(("row", "col"), None),
            P(("row", "col"), None),
            P(("row", "col"), None, None, None, None),
            P(("row", "col"), None, None, None, None),
            P(),
            P(),
            P(),
        ),
        out_specs=(P(("row", "col"), None), P(("row", "col"), None)),
        check_vma=False,
    )
```

```python
import math

import jax
import jax.numpy as jnp
from jax import lax
from jax.experimental import pallas as pl
from jax.experimental.pallas import tpu as pltpu
from jax.sharding import PartitionSpec as P

EPSILON = 1e-06
F32 = jnp.float32
BF16 = jnp.bfloat16
I32 = jnp.int32
ROWS = 16
COLS = 8
N = 128
D = 3584
HEADS = 14
GROUP = 7
DH = 128
PARENTS = 32
BLOCK = 128
DELTA_HALVES = (512, 512, 384, 384)
DELTA_STARTS = (0, 1024, 2048, 2816)
DELTA_CHUNKS = 4
BACK_TILES = (4, 3, 2)
BACK_STARTS = (0, 4, 7)
BACK_CHUNKS = 3
SHARE_CHUNKS = 2
KEYS = 512
TILES = 4
TILE = GROUP * N * 2 // TILES
PAIRS = 8
SIDE = N // 2
EXCLUDED = -1e30
SCORE_SCALE = math.log2(math.e) / math.sqrt(DH)


def iotas(shape):
    return lax.broadcasted_iota(I32, shape, 0), lax.broadcasted_iota(I32, shape, 1)


def one_zero(mask, kind=BF16):
    return jnp.where(mask, 1.0, 0.0).astype(kind)


def to_col(row):
    below, along = iotas((N, N))
    return jnp.sum(jnp.where(below == along, row, 0.0), axis=1, keepdims=True)


def to_row(col):
    below, along = iotas((N, N))
    return jnp.sum(jnp.where(below == along, col, 0.0), axis=0, keepdims=True)


def rank_row(key_row, key_col):
    below, along = iotas((N, N))
    earlier = (key_col == key_row) & (below < along)
    return jnp.sum(jnp.where(earlier, 1.0, 0.0), axis=0, keepdims=True)


def column_order(ids):
    column = ((ids >> 5) & (COLS - 1)).astype(F32)
    return column * 16.0 + rank_row(column, to_col(column))


def dot(a, b):
    return jnp.dot(a, b, preferred_element_type=F32)


def dot_t(a, b):
    return lax.dot_general(a, b, (((1,), (1,)), ((), ())), preferred_element_type=F32)


def pair_rows(left, right):
    width = left.shape[1]
    both = jnp.concatenate(
        [left.reshape(ROWS, 1, 8, width), right.reshape(ROWS, 1, 8, width)], axis=1
    )
    return both.reshape(2 * N, width)


class Exchange:
    def __init__(self, axis, count, me, rows):
        self.axis, self.count, self.me, self.rows = axis, count, me, rows

    def part(self, ref, k):
        return ref.at[pl.ds(pl.multiple_of(k * self.rows, self.rows), self.rows)]

    def copy(self, src, dst, send, recv, k, slot):
        return pltpu.make_async_remote_copy(
            src_ref=self.part(src, k),
            dst_ref=self.part(dst, slot),
            send_sem=send.at[k],
            recv_sem=recv.at[slot],
            device_id={self.axis: k},
            device_id_type=pl.DeviceIdType.MESH,
        )

    def each(self, act):
        def body(k, carry):
            act(lax.rem(self.me + k, self.count))
            return carry

        lax.fori_loop(1, self.count, body, 0)

    def start(self, src, dst, send, recv):
        self.each(lambda k: self.copy(src, dst, send, recv, k, self.me).start())
        own = pl.ds(pl.multiple_of(self.me * self.rows, self.rows), self.rows)
        dst[own, :] = src[own, :]

    def arrived(self, src, dst, send, recv):
        self.each(lambda k: self.copy(src, dst, send, recv, k, k).wait_recv())

    def sent(self, src, dst, send, recv):
        self.each(lambda k: self.copy(src, dst, send, recv, k, self.me).wait_send())


def layer_kernel(
    ids_ref,
    lens_ref,
    gain_ref,
    delta_hbm,
    hidden_hbm,
    blocks_hbm,
    wq_hbm,
    wkv_hbm,
    prefix_hbm,
    context_ref,
    kv_ref,
    delta_v,
    hidden_v,
    blocks_v,
    weight_v,
    out1,
    in1,
    out2,
    in2,
    id_out1,
    id_in1,
    id_out2,
    id_in2,
    normed,
    heads_v,
    back1,
    back1_in,
    back2,
    prob,
    stat,
    share1,
    share1_in,
    share2,
    back_in,
    share_in,
    prefix_v,
    block_v,
    query_v,
    near_score,
    near_total,
    near_top,
    kv_v,
    context_v,
    save_sem,
    load_sem,
    d1s,
    d1r,
    d2s,
    d2r,
    i1s,
    i1r,
    i2s,
    i2r,
    b1s,
    b1r,
    b2s,
    b2r,
    s1s,
    s1r,
    s2s,
    s2r,
):
    my_row = lax.axis_index("row")
    my_col = lax.axis_index("col")
    load_delta = pltpu.make_async_copy(delta_hbm, delta_v, load_sem.at[0])
    load_delta.start()

    barrier = pltpu.get_barrier_semaphore()

    def greet_col(k, carry):
        pl.semaphore_signal(
            barrier,
            inc=1,
            device_id={"col": lax.rem(my_col + k, COLS)},
            device_id_type=pl.DeviceIdType.MESH,
        )
        return carry

    def greet_row(k, carry):
        pl.semaphore_signal(
            barrier,
            inc=1,
            device_id={"row": lax.rem(my_row + k, ROWS)},
            device_id_type=pl.DeviceIdType.MESH,
        )
        return carry

    lax.fori_loop(1, COLS, greet_col, 0)
    lax.fori_loop(1, ROWS, greet_row, 0)

    below, along = iotas((N, N))
    ids = ids_ref[...]
    order = column_order(ids)
    pick = order == below.astype(F32)
    sorting = one_zero(pick)
    far_row = (ids >> 8).astype(F32)
    far_local = (ids & (PARENTS - 1)).astype(F32)
    row_sorted = jnp.sum(jnp.where(pick, far_row, 0.0), axis=1, keepdims=True)
    local_sorted = jnp.sum(jnp.where(pick, far_local, 0.0), axis=1, keepdims=True)
    id_out1[...] = jnp.where(along < 64, row_sorted, local_sorted).astype(BF16)

    loads = [
        pltpu.make_async_copy(hidden_hbm, hidden_v, load_sem.at[1]),
        pltpu.make_async_copy(wq_hbm, weight_v.at[:, pl.ds(0, HEADS * DH)], load_sem.at[2]),
        pltpu.make_async_copy(wkv_hbm, weight_v.at[:, pl.ds(HEADS * DH, 512)], load_sem.at[3]),
        pltpu.make_async_copy(blocks_hbm, blocks_v, load_sem.at[4]),
        pltpu.make_async_copy(prefix_hbm, prefix_v, load_sem.at[5]),
    ]
    load_delta.wait()
    for load in loads:
        load.start()
    order_col = to_col(order)
    unsort = one_zero(order_col == along.astype(F32))
    lens_col = to_col(lens_ref[...].astype(F32))
    bias = jnp.where(along.astype(F32) < lens_col, 0.0, EXCLUDED).astype(BF16)

    by_col = Exchange("col", COLS, my_col, 16)
    by_row = Exchange("row", ROWS, my_row, 16)
    by_row8 = Exchange("row", ROWS, my_row, 8)

    pl.semaphore_wait(barrier, COLS + ROWS - 2)
    by_col.start(id_out1, id_in1, i1s, i1r)
    for c in range(DELTA_CHUNKS):
        first = DELTA_STARTS[c]
        out1[c][...] = dot(sorting, delta_v[:, first : first + 2 * DELTA_HALVES[c]]).astype(BF16)
        by_col.start(out1[c], in1[c], d1s.at[c], d1r.at[c])

    wide = near_score.at[0:N, 0:D]
    score = near_score.at[N : 2 * N, 0 : 2 * HEADS * DH]
    total = near_score.at[2 * N : 3 * N, 0 : 2 * HEADS * DH]
    score[...] = jnp.zeros(score.shape, F32)
    total[...] = jnp.zeros(total.shape, F32)
    def store_query(h, lanes, value):
        at = (h % GROUP) * SIDE
        for side in range(2):
            query_v[(h // GROUP) * 2 + side, at : at + SIDE, lanes] = value[
                side * SIDE : (side + 1) * SIDE
            ]

    for h in range(HEADS):
        store_query(h, slice(DH, 2 * DH), bias)
    for b in range(prefix_v.shape[2] // BLOCK):
        block_v[b * BLOCK : (b + 1) * BLOCK] = one_zero(along == b)

    by_col.arrived(id_out1, id_in1, i1s, i1r)
    arrived_ids = id_in1[...].astype(F32)
    row_col = arrived_ids[:, 0:1]
    row_row = to_row(row_col)
    local_row = to_row(arrived_ids[:, 64:65])
    place = row_row * 8.0 + rank_row(row_row, row_col)
    place_col = to_col(place)
    place_pick = place == below.astype(F32)
    id_out2[...] = jnp.broadcast_to(
        jnp.sum(jnp.where(place_pick, local_row, 0.0), axis=1, keepdims=True), (N, N)
    )
    by_row8.start(id_out2, id_in2, i2s, i2r)

    wide_below, wide_along = iotas((2 * N, 2 * N))
    code_below = ((wide_below >> 4) * 16 + (wide_below & 7) * 2 + ((wide_below >> 3) & 1)).astype(
        F32
    )
    code_along = ((wide_along >> 4) * 16 + (wide_along & 7) * 2 + ((wide_along >> 3) & 1)).astype(
        F32
    )
    code_row = jnp.concatenate([place * 2.0, place * 2.0 + 1.0], axis=1)
    code_col = jnp.concatenate([place_col * 2.0, place_col * 2.0 + 1.0], axis=0)
    forth = one_zero(code_below == code_row)
    turn = one_zero(code_along == code_col)

    for c in range(DELTA_CHUNKS):
        by_col.arrived(out1[c], in1[c], d1s.at[c], d1r.at[c])
        width = DELTA_HALVES[c]
        stacked = jnp.concatenate([in1[c][:, :width], in1[c][:, width:]], axis=0)
        out2[c][...] = dot(forth, stacked).astype(BF16)
        by_row.start(out2[c], in2[c], d2s.at[c], d2r.at[c])

    loads[0].wait()
    by_row8.arrived(id_out2, id_in2, i2s, i2r)
    local_id = id_in2[...]
    owner = one_zero(local_id[:, :PARENTS] == along[:, :PARENTS].astype(F32))
    squares = jnp.zeros((N, 1), F32)
    for c in range(DELTA_CHUNKS):
        by_row.arrived(out2[c], in2[c], d2s.at[c], d2r.at[c])
        for half in range(2):
            for w in range(DELTA_HALVES[c] // 128):
                at = DELTA_STARTS[c] + half * DELTA_HALVES[c] + w * 128
                grid = in2[c][:, w * 128 : (w + 1) * 128].astype(F32)
                grid = grid.reshape(ROWS, 2, 8, 128)[:, half].reshape(N, 128)
                value = dot(owner, hidden_v[:, at : at + 128]) + grid
                wide[:, at : at + 128] = value
                squares = squares + jnp.sum(value * value, axis=1, keepdims=True)
    inverse = lax.rsqrt(squares / D + EPSILON)
    for w in range(D // 128):
        at = w * 128
        normed[:, at : at + 128] = (
            wide[:, at : at + 128] * inverse * gain_ref[w : w + 1]
        ).astype(BF16)

    loads[1].wait()
    loads[2].wait()
    for c in range(BACK_CHUNKS):

        def project(t, carry, c=c):
            n = BACK_STARTS[c] + t
            y = dot(normed[...], weight_v[:, pl.ds(pl.multiple_of(n * 256, 256), 256)])
            heads_v[2 * n] = y[:, :128].astype(BF16)
            heads_v[2 * n + 1] = y[:, 128:].astype(BF16)
            back1[c][:, pl.ds(pl.multiple_of(t * 128, 128), 128)] = pair_rows(
                y[:, :128], y[:, 128:]
            ).astype(BF16)
            return carry

        lax.fori_loop(0, BACK_TILES[c], project, 0)
        by_row.start(back1[c], back1_in[c], b1s.at[c], b1r.at[c])

    loads[3].wait()

    def pass_back(c):
        by_row.arrived(back1[c], back1_in[c], b1s.at[c], b1r.at[c])
        turned = dot(turn, back1_in[c][...]).astype(BF16)
        for t in range(BACK_TILES[c]):
            back2[c][:, t * 256 : t * 256 + 128] = turned[:N, t * 128 : (t + 1) * 128]
            back2[c][:, t * 256 + 128 : (t + 1) * 256] = turned[N:, t * 128 : (t + 1) * 128]
        by_col.start(back2[c], back_in[c], b2s.at[c], b2r.at[c])

    def masked(source, g, masks):
        return jnp.concatenate(
            [
                jnp.concatenate([source[g * GROUP + h] * mask for mask in masks], axis=1)
                for h in range(GROUP)
            ],
            axis=0,
        )

    pair_id = jnp.floor(local_id * 0.5)
    second = local_id != pair_id * 2.0

    def masks_of(k):
        return [one_zero(pair_id == (PAIRS * k + i).astype(F32)) for i in range(PAIRS)]

    def add_heads(target, g, value):
        for h in range(GROUP):
            at = (g * GROUP + h) * 2 * DH
            target[:, at : at + 2 * DH] += value[h * N : (h + 1) * N]

    def blocks_of(k, kind, g, side, axis):
        return jnp.concatenate(
            [blocks_v[2 * (PAIRS * k + i) + side, kind, g] for i in range(PAIRS)], axis=axis
        )

    def score_step(k, carry):
        masks = masks_of(k)
        for g in range(2):
            keys = jnp.concatenate([blocks_of(k, 0, g, side, 1) for side in range(2)], axis=0)
            add_heads(score, g, dot_t(masked(heads_v, g, masks), keys))
        return carry

    def value_step(k, carry):
        masks = masks_of(k)
        for g in range(2):
            values = jnp.concatenate([blocks_of(k, 1, g, side, 0) for side in range(2)], axis=1)
            add_heads(total, g, dot(masked(prob, g, masks), values))
        return carry

    def side_of(source, i):
        at = i * 2 * DH
        return jnp.where(second, source[:, at + DH : at + 2 * DH], source[:, at : at + DH])

    lax.fori_loop(0, 1, score_step, 0)
    pass_back(0)
    lax.fori_loop(1, 2, score_step, 0)
    pass_back(1)

    for g in range(2):
        stats = jnp.zeros((N, N), F32)
        for h in range(GROUP):
            s = side_of(score, g * GROUP + h) * SCORE_SCALE
            top = jnp.max(s, axis=1, keepdims=True)
            e = jnp.exp2(s - top)
            prob[g * GROUP + h] = e.astype(BF16)
            stats = jnp.where(along == h, top, stats)
            stats = jnp.where(along == 8 + h, jnp.sum(e, axis=1, keepdims=True), stats)
        stat[g] = stats

    lax.fori_loop(0, 1, value_step, 0)
    pass_back(2)
    lax.fori_loop(1, 2, value_step, 0)

    for c in range(SHARE_CHUNKS):
        for b in range(4):
            h = c * 4 + b
            sides = []
            for g in range(2):
                stats = stat[g]
                if h < GROUP:
                    sides.append(side_of(total, g * GROUP + h) / stats[:, 8 + h : 9 + h])
                else:
                    high = stats.astype(BF16).astype(F32)
                    rest = stats - high
                    middle = rest.astype(BF16).astype(F32)
                    low = rest - middle
                    sides.append(
                        high + pltpu.roll(middle, shift=16, axis=1) + pltpu.roll(low, shift=32, axis=1)
                    )
            share1[c, :, b * 128 : (b + 1) * 128] = pair_rows(sides[0], sides[1]).astype(BF16)
        by_row.start(share1.at[c], share1_in.at[c], s1s.at[c], s1r.at[c])

    def take_back(c):
        by_col.arrived(back2[c], back_in[c], b2s.at[c], b2r.at[c])
        own = dot(unsort, back_in[c][...]).astype(BF16)
        for t in range(BACK_TILES[c]):
            n = BACK_STARTS[c] + t
            if n < GROUP:
                for half in range(2):
                    store_query(2 * n + half, slice(0, DH), own[:, t * 256 + half * 128 :][:, :DH])
            else:
                kv_v[:, (n - GROUP) * 256 : (n - GROUP + 1) * 256] = own[
                    :, t * 256 : (t + 1) * 256
                ]

    take_back(0)
    loads[4].wait()
    spans = [slice(k, k + KEYS) for k in range(0, prefix_v.shape[2], KEYS)]
    ones = jnp.ones((KEYS, DH), BF16)

    def near_scores(q, g, span, top):
        keys = jnp.concatenate([prefix_v[0, g, span], block_v[span]], axis=1)
        part = dot_t(q, keys)
        near_score[:, span] = part
        for w in range(KEYS // 128):
            top = jnp.maximum(top, part[:, w * 128 : (w + 1) * 128])
        return top

    def near_values(top, g, span, sums):
        e = jnp.exp2(near_score[:, span] * SCORE_SCALE - top).astype(BF16)
        return sums + dot(e, jnp.concatenate([prefix_v[1, g, span], ones], axis=1))

    def keep_top(t, top):
        near_top[t] = jnp.broadcast_to(
            jnp.max(top, axis=1, keepdims=True) * SCORE_SCALE, (TILE, DH)
        )

    def tile(t, carry):
        later = t + 1
        q = query_v[later]
        top = near_top[t][:, :1]
        next_top = jnp.full((TILE, DH), EXCLUDED, F32)
        sums = jnp.zeros((TILE, 2 * DH), F32)
        for span in spans:
            sums = near_values(top, t // 2, span, sums)
            next_top = near_scores(q, later // 2, span, next_top)
        near_total[t] = sums
        keep_top(later, next_top)
        return carry

    first_top = jnp.full((TILE, DH), EXCLUDED, F32)
    for span in spans:
        first_top = near_scores(query_v[0], 0, span, first_top)
    keep_top(0, first_top)
    lax.fori_loop(0, 1, tile, 0)
    take_back(1)

    for c in range(SHARE_CHUNKS):
        by_row.arrived(share1.at[c], share1_in.at[c], s1s.at[c], s1r.at[c])
        turned = dot(turn, share1_in[c]).astype(BF16)
        share2[c, :, :512] = turned[:N]
        share2[c, :, 512:] = turned[N:]
        by_col.start(share2.at[c], share_in.at[c], s2s.at[c], s2r.at[c])

    lax.fori_loop(1, TILES - 1, tile, 0)
    take_back(2)
    save_kv = pltpu.make_async_copy(kv_v, kv_ref, save_sem.at[2])
    save_kv.start()
    last_top = near_top[TILES - 1][:, :1]
    last_sums = jnp.zeros((TILE, 2 * DH), F32)
    for span in spans:
        last_sums = near_values(last_top, 1, span, last_sums)
    near_total[TILES - 1] = last_sums

    for c in range(SHARE_CHUNKS):
        by_col.arrived(share2.at[c], share_in.at[c], s2s.at[c], s2r.at[c])
    saves = [save_kv]
    for g in range(2):
        packed = dot(unsort, share_in[1, :, g * 512 + 384 : g * 512 + 512])
        stats = (
            packed
            + pltpu.roll(packed, shift=N - 16, axis=1)
            + pltpu.roll(packed, shift=N - 32, axis=1)
        )
        for h in range(GROUP):
            c, b = h // 4, h % 4
            i = g * GROUP + h
            part = dot(unsort, share_in[c, :, g * 512 + b * 128 : g * 512 + (b + 1) * 128])
            top_far = stats[:, h : h + 1]
            mass_far = stats[:, 8 + h : 9 + h]
            rows = slice(h * SIDE, (h + 1) * SIDE)
            top_near = jnp.concatenate([near_top[2 * g, rows], near_top[2 * g + 1, rows]], axis=0)
            top = jnp.maximum(top_near, top_far)
            near = jnp.exp2(top_near - top)
            far = jnp.exp2(top_far - top) * mass_far
            sums = jnp.concatenate([near_total[2 * g, rows], near_total[2 * g + 1, rows]], axis=0)
            whole = sums[:, DH:] * near + far
            context_v[:, i * DH : (i + 1) * DH] = (
                (sums[:, :DH] * near + part * far) / whole
            ).astype(BF16)

        lanes = pl.ds(g * GROUP * DH, GROUP * DH)
        save = pltpu.make_async_copy(
            context_v.at[:, lanes], context_ref.at[:, lanes], save_sem.at[g]
        )
        save.start()
        saves.append(save)

    by_col.sent(id_out1, id_in1, i1s, i1r)
    by_row8.sent(id_out2, id_in2, i2s, i2r)
    for c in range(DELTA_CHUNKS):
        by_col.sent(out1[c], in1[c], d1s.at[c], d1r.at[c])
        by_row.sent(out2[c], in2[c], d2s.at[c], d2r.at[c])
    for c in range(BACK_CHUNKS):
        by_row.sent(back1[c], back1_in[c], b1s.at[c], b1r.at[c])
        by_col.sent(back2[c], back_in[c], b2s.at[c], b2r.at[c])
    for c in range(SHARE_CHUNKS):
        by_row.sent(share1.at[c], share1_in.at[c], s1s.at[c], s1r.at[c])
        by_col.sent(share2.at[c], share_in.at[c], s2s.at[c], s2r.at[c])
    for save in saves:
        save.wait()


def result_kernel(context_in, kv_in, context_ref, kv_ref, context_v, kv_v, sem):
    top, bottom = pl.ds(0, SIDE), pl.ds(SIDE, SIDE)
    hops = [
        (context_in.at[top], context_v.at[top], context_ref.at[top]),
        (context_in.at[bottom], context_v.at[bottom], context_ref.at[bottom]),
        (kv_in, kv_v, kv_ref),
    ]
    fetches = [pltpu.make_async_copy(h[0], h[1], sem.at[0, i]) for i, h in enumerate(hops)]
    stores = [pltpu.make_async_copy(h[1], h[2], sem.at[1, i]) for i, h in enumerate(hops)]
    for fetch in fetches:
        fetch.start()
    for fetch, store in zip(fetches, stores):
        fetch.wait()
        store.start()
    for store in stores:
        store.wait()


def local(
    child_parent,
    prefix_len,
    child_delta,
    parent_hidden,
    parent_cache,
    prefix_cache,
    norm_gain,
    w_query,
    w_kv,
):
    vmem = pl.BlockSpec(memory_space=pltpu.VMEM)
    hbm = pl.BlockSpec(memory_space=pl.ANY)
    dma = pltpu.SemaphoreType.DMA
    ids = child_parent.reshape(1, N)
    lens = prefix_len.reshape(1, N)
    tokens = prefix_cache.shape[3]
    share_shape = (SHARE_CHUNKS, N, 1024)
    results = (
        jax.ShapeDtypeStruct((N, HEADS * DH), BF16),
        jax.ShapeDtypeStruct((N, 512), BF16),
    )
    context, new_kv = pl.pallas_call(
        layer_kernel,
        name="decode_layer",
        out_shape=results,
        in_specs=[vmem, vmem, vmem, hbm, hbm, hbm, hbm, hbm, hbm],
        out_specs=(hbm, hbm),
        scratch_shapes=[
            pltpu.VMEM((N, D), BF16),
            pltpu.VMEM((PARENTS, D), BF16),
            pltpu.VMEM((PARENTS, 2, 2, BLOCK, DH), BF16),
            pltpu.VMEM((D, 2304), BF16),
            [pltpu.VMEM((N, 2 * half), BF16) for half in DELTA_HALVES],
            [pltpu.VMEM((N, 2 * half), BF16) for half in DELTA_HALVES],
            [pltpu.VMEM((2 * N, half), BF16) for half in DELTA_HALVES],
            [pltpu.VMEM((2 * N, half), BF16) for half in DELTA_HALVES],
            pltpu.VMEM((N, N), BF16),
            pltpu.VMEM((N, N), BF16),
            pltpu.VMEM((N, N), F32),
            pltpu.VMEM((N, N), F32),
            pltpu.VMEM((N, D), BF16),
            pltpu.VMEM((18, N, 128), BF16),
            [pltpu.VMEM((2 * N, tiles * 128), BF16) for tiles in BACK_TILES],
            [pltpu.VMEM((2 * N, tiles * 128), BF16) for tiles in BACK_TILES],
            [pltpu.VMEM((N, tiles * 256), BF16) for tiles in BACK_TILES],
            pltpu.VMEM((HEADS, N, BLOCK), BF16),
            pltpu.VMEM((2, N, N), F32),
            pltpu.VMEM((SHARE_CHUNKS, 2 * N, 512), BF16),
            pltpu.VMEM((SHARE_CHUNKS, 2 * N, 512), BF16),
            pltpu.VMEM(share_shape, BF16),
            [pltpu.VMEM((N, tiles * 256), BF16) for tiles in BACK_TILES],
            pltpu.VMEM(share_shape, BF16),
            pltpu.VMEM((2, 2, tokens, DH), BF16),
            pltpu.VMEM((tokens, BLOCK), BF16),
            pltpu.VMEM((TILES, TILE, 2 * DH), BF16),
            pltpu.VMEM((TILE, tokens), F32),
            pltpu.VMEM((TILES, TILE, 2 * DH), F32),
            pltpu.VMEM((TILES, TILE, DH), F32),
            pltpu.VMEM((N, 512), BF16),
            pltpu.VMEM((N, HEADS * DH), BF16),
            dma((3,)),
            dma((6,)),
            dma((DELTA_CHUNKS, COLS)),
            dma((DELTA_CHUNKS, COLS)),
            dma((DELTA_CHUNKS, ROWS)),
            dma((DELTA_CHUNKS, ROWS)),
            dma((COLS,)),
            dma((COLS,)),
            dma((ROWS,)),
            dma((ROWS,)),
            dma((BACK_CHUNKS, ROWS)),
            dma((BACK_CHUNKS, ROWS)),
            dma((BACK_CHUNKS, COLS)),
            dma((BACK_CHUNKS, COLS)),
            dma((SHARE_CHUNKS, ROWS)),
            dma((SHARE_CHUNKS, ROWS)),
            dma((SHARE_CHUNKS, COLS)),
            dma((SHARE_CHUNKS, COLS)),
        ],
        compiler_params=pltpu.CompilerParams(
            collective_id=0, has_side_effects=True, vmem_limit_bytes=60 << 20
        ),
    )(
        ids,
        lens,
        norm_gain.reshape(D // 128, 128),
        child_delta,
        parent_hidden,
        parent_cache,
        w_query,
        w_kv,
        prefix_cache.reshape(prefix_cache.shape[1:]),
    )
    return pl.pallas_call(
        result_kernel,
        name="results",
        out_shape=results,
        in_specs=[hbm, hbm],
        out_specs=(hbm, hbm),
        scratch_shapes=[
            pltpu.VMEM((N, HEADS * DH), BF16),
            pltpu.VMEM((N, 512), BF16),
            dma((2, 3)),
        ],
        compiler_params=pltpu.CompilerParams(vmem_limit_bytes=60 << 20),
    )(context, new_kv)


def solution(mesh):
    return jax.shard_map(
        local,
        mesh=mesh,
        in_specs=(
            P(("row", "col")),
            P(("row", "col")),
            P(("row", "col"), None),
            P(("row", "col"), None),
            P(("row", "col"), None, None, None, None),
            P(("row", "col"), None, None, None, None),
            P(),
            P(),
            P(),
        ),
        out_specs=(P(("row", "col"), None), P(("row", "col"), None)),
        check_vma=False,
    )
```

```python
import math

import jax
import jax.numpy as jnp
from jax import lax
from jax.experimental import pallas as pl
from jax.experimental.pallas import tpu as pltpu
from jax.sharding import PartitionSpec as P

EPSILON = 1e-06
F32 = jnp.float32
BF16 = jnp.bfloat16
I32 = jnp.int32
ROWS = 16
COLS = 8
N = 128
D = 3584
HEADS = 14
GROUP = 7
DH = 128
PARENTS = 32
BLOCK = 128
DELTA_HALVES = (512, 512, 384, 384)
DELTA_STARTS = (0, 1024, 2048, 2816)
DELTA_CHUNKS = 4
BACK_TILES = (4, 3, 2)
BACK_STARTS = (0, 4, 7)
BACK_CHUNKS = 3
SHARE_CHUNKS = 2
KEYS = 512
TILES = 4
TILE = GROUP * N * 2 // TILES
PAIRS = 8
SIDE = N // 2
EXCLUDED = -1e30
SCORE_SCALE = math.log2(math.e) / math.sqrt(DH)


def iotas(shape):
    return lax.broadcasted_iota(I32, shape, 0), lax.broadcasted_iota(I32, shape, 1)


def one_zero(mask, kind=BF16):
    return jnp.where(mask, 1.0, 0.0).astype(kind)


def to_col(row):
    below, along = iotas((N, N))
    return jnp.sum(jnp.where(below == along, row, 0.0), axis=1, keepdims=True)


def to_row(col):
    below, along = iotas((N, N))
    return jnp.sum(jnp.where(below == along, col, 0.0), axis=0, keepdims=True)


def rank_row(key_row, key_col):
    below, along = iotas((N, N))
    earlier = (key_col == key_row) & (below < along)
    return jnp.sum(jnp.where(earlier, 1.0, 0.0), axis=0, keepdims=True)


def column_order(ids):
    column = ((ids >> 5) & (COLS - 1)).astype(F32)
    return column * 16.0 + rank_row(column, to_col(column))


def dot(a, b):
    return jnp.dot(a, b, preferred_element_type=F32)


def dot_t(a, b):
    return lax.dot_general(a, b, (((1,), (1,)), ((), ())), preferred_element_type=F32)


def pair_rows(left, right):
    width = left.shape[1]
    both = jnp.concatenate(
        [left.reshape(ROWS, 1, 8, width), right.reshape(ROWS, 1, 8, width)], axis=1
    )
    return both.reshape(2 * N, width)


class Exchange:
    def __init__(self, axis, count, me, rows):
        self.axis, self.count, self.me, self.rows = axis, count, me, rows

    def part(self, ref, k):
        return ref.at[pl.ds(pl.multiple_of(k * self.rows, self.rows), self.rows)]

    def copy(self, src, dst, send, recv, k, slot):
        return pltpu.make_async_remote_copy(
            src_ref=self.part(src, k),
            dst_ref=self.part(dst, slot),
            send_sem=send,
            recv_sem=recv,
            device_id={self.axis: k},
            device_id_type=pl.DeviceIdType.MESH,
        )

    def whole(self, src, dst, send, recv):
        rows = pl.ds(0, (self.count - 1) * self.rows)
        return pltpu.make_async_remote_copy(
            src_ref=src.at[rows],
            dst_ref=dst.at[rows],
            send_sem=send,
            recv_sem=recv,
            device_id={self.axis: lax.rem(self.me + 1, self.count)},
            device_id_type=pl.DeviceIdType.MESH,
        )

    def start(self, src, dst, send, recv):
        def body(k, carry):
            self.copy(src, dst, send, recv, lax.rem(self.me + k, self.count), self.me).start()
            return carry

        lax.fori_loop(1, self.count, body, 0)
        own = pl.ds(pl.multiple_of(self.me * self.rows, self.rows), self.rows)
        dst[own, :] = src[own, :]

    def arrived(self, src, dst, send, recv):
        self.whole(src, dst, send, recv).wait_recv()

    def sent(self, src, dst, send, recv):
        self.whole(src, dst, send, recv).wait_send()


def layer_kernel(
    ids_ref,
    lens_ref,
    gain_ref,
    delta_hbm,
    hidden_hbm,
    blocks_hbm,
    wq_hbm,
    wkv_hbm,
    prefix_hbm,
    context_ref,
    kv_ref,
    delta_v,
    hidden_v,
    blocks_v,
    weight_v,
    out1,
    in1,
    out2,
    in2,
    id_out1,
    id_in1,
    id_out2,
    id_in2,
    normed,
    heads_v,
    back1,
    back1_in,
    back2,
    prob,
    stat,
    share1,
    share1_in,
    share2,
    back_in,
    share_in,
    prefix_v,
    block_v,
    query_v,
    near_score,
    near_total,
    near_top,
    kv_v,
    context_v,
    save_sem,
    load_sem,
    d1s,
    d1r,
    d2s,
    d2r,
    i1s,
    i1r,
    i2s,
    i2r,
    b1s,
    b1r,
    b2s,
    b2r,
    s1s,
    s1r,
    s2s,
    s2r,
):
    my_row = lax.axis_index("row")
    my_col = lax.axis_index("col")
    load_delta = pltpu.make_async_copy(delta_hbm, delta_v, load_sem.at[0])
    load_delta.start()

    barrier = pltpu.get_barrier_semaphore()

    def greet_col(k, carry):
        pl.semaphore_signal(
            barrier,
            inc=1,
            device_id={"col": lax.rem(my_col + k, COLS)},
            device_id_type=pl.DeviceIdType.MESH,
        )
        return carry

    def greet_row(k, carry):
        pl.semaphore_signal(
            barrier,
            inc=1,
            device_id={"row": lax.rem(my_row + k, ROWS)},
            device_id_type=pl.DeviceIdType.MESH,
        )
        return carry

    lax.fori_loop(1, COLS, greet_col, 0)
    lax.fori_loop(1, ROWS, greet_row, 0)

    below, along = iotas((N, N))
    ids = ids_ref[...]
    order = column_order(ids)
    pick = order == below.astype(F32)
    sorting = one_zero(pick)
    far_row = (ids >> 8).astype(F32)
    far_local = (ids & (PARENTS - 1)).astype(F32)
    row_sorted = jnp.sum(jnp.where(pick, far_row, 0.0), axis=1, keepdims=True)
    local_sorted = jnp.sum(jnp.where(pick, far_local, 0.0), axis=1, keepdims=True)
    id_out1[...] = jnp.where(along < 64, row_sorted, local_sorted).astype(BF16)

    loads = [
        pltpu.make_async_copy(hidden_hbm, hidden_v, load_sem.at[1]),
        pltpu.make_async_copy(wq_hbm, weight_v.at[:, pl.ds(0, HEADS * DH)], load_sem.at[2]),
        pltpu.make_async_copy(wkv_hbm, weight_v.at[:, pl.ds(HEADS * DH, 512)], load_sem.at[3]),
        pltpu.make_async_copy(blocks_hbm, blocks_v, load_sem.at[4]),
        pltpu.make_async_copy(prefix_hbm, prefix_v, load_sem.at[5]),
    ]
    load_delta.wait()
    for load in loads:
        load.start()
    order_col = to_col(order)
    unsort = one_zero(order_col == along.astype(F32))
    lens_col = to_col(lens_ref[...].astype(F32))
    bias = jnp.where(along.astype(F32) < lens_col, 0.0, EXCLUDED).astype(BF16)

    by_col = Exchange("col", COLS, my_col, 16)
    by_row = Exchange("row", ROWS, my_row, 16)
    by_row8 = Exchange("row", ROWS, my_row, 8)

    pl.semaphore_wait(barrier, COLS + ROWS - 2)
    by_col.start(id_out1, id_in1, i1s, i1r)
    for c in range(DELTA_CHUNKS):
        first = DELTA_STARTS[c]
        out1[c][...] = dot(sorting, delta_v[:, first : first + 2 * DELTA_HALVES[c]]).astype(BF16)
        by_col.start(out1[c], in1[c], d1s.at[c], d1r.at[c])

    wide = near_score.at[0:N, 0:D]
    score = near_score.at[N : 2 * N, 0 : 2 * HEADS * DH]
    total = near_score.at[2 * N : 3 * N, 0 : 2 * HEADS * DH]
    score[...] = jnp.zeros(score.shape, F32)
    total[...] = jnp.zeros(total.shape, F32)
    def store_query(h, lanes, value):
        at = (h % GROUP) * SIDE
        for side in range(2):
            query_v[(h // GROUP) * 2 + side, at : at + SIDE, lanes] = value[
                side * SIDE : (side + 1) * SIDE
            ]

    for h in range(HEADS):
        store_query(h, slice(DH, 2 * DH), bias)
    for b in range(prefix_v.shape[2] // BLOCK):
        block_v[b * BLOCK : (b + 1) * BLOCK] = one_zero(along == b)

    by_col.arrived(id_out1, id_in1, i1s, i1r)
    arrived_ids = id_in1[...].astype(F32)
    row_col = arrived_ids[:, 0:1]
    row_row = to_row(row_col)
    local_row = to_row(arrived_ids[:, 64:65])
    place = row_row * 8.0 + rank_row(row_row, row_col)
    place_col = to_col(place)
    place_pick = place == below.astype(F32)
    id_out2[...] = jnp.broadcast_to(
        jnp.sum(jnp.where(place_pick, local_row, 0.0), axis=1, keepdims=True), (N, N)
    )
    by_row8.start(id_out2, id_in2, i2s, i2r)

    wide_below, wide_along = iotas((2 * N, 2 * N))
    code_below = ((wide_below >> 4) * 16 + (wide_below & 7) * 2 + ((wide_below >> 3) & 1)).astype(
        F32
    )
    code_along = ((wide_along >> 4) * 16 + (wide_along & 7) * 2 + ((wide_along >> 3) & 1)).astype(
        F32
    )
    code_row = jnp.concatenate([place * 2.0, place * 2.0 + 1.0], axis=1)
    code_col = jnp.concatenate([place_col * 2.0, place_col * 2.0 + 1.0], axis=0)
    forth = one_zero(code_below == code_row)
    turn = one_zero(code_along == code_col)

    for c in range(DELTA_CHUNKS):
        by_col.arrived(out1[c], in1[c], d1s.at[c], d1r.at[c])
        width = DELTA_HALVES[c]
        stacked = jnp.concatenate([in1[c][:, :width], in1[c][:, width:]], axis=0)
        out2[c][...] = dot(forth, stacked).astype(BF16)
        by_row.start(out2[c], in2[c], d2s.at[c], d2r.at[c])

    loads[0].wait()
    by_row8.arrived(id_out2, id_in2, i2s, i2r)
    local_id = id_in2[...]
    owner = one_zero(local_id[:, :PARENTS] == along[:, :PARENTS].astype(F32))
    squares = jnp.zeros((N, 1), F32)
    for c in range(DELTA_CHUNKS):
        by_row.arrived(out2[c], in2[c], d2s.at[c], d2r.at[c])
        for half in range(2):
            for w in range(DELTA_HALVES[c] // 128):
                at = DELTA_STARTS[c] + half * DELTA_HALVES[c] + w * 128
                grid = in2[c][:, w * 128 : (w + 1) * 128].astype(F32)
                grid = grid.reshape(ROWS, 2, 8, 128)[:, half].reshape(N, 128)
                value = dot(owner, hidden_v[:, at : at + 128]) + grid
                wide[:, at : at + 128] = value
                squares = squares + jnp.sum(value * value, axis=1, keepdims=True)
    inverse = lax.rsqrt(squares / D + EPSILON)
    for w in range(D // 128):
        at = w * 128
        normed[:, at : at + 128] = (
            wide[:, at : at + 128] * inverse * gain_ref[w : w + 1]
        ).astype(BF16)

    loads[1].wait()
    loads[2].wait()
    for c in range(BACK_CHUNKS):

        def project(t, carry, c=c):
            n = BACK_STARTS[c] + t
            y = dot(normed[...], weight_v[:, pl.ds(pl.multiple_of(n * 256, 256), 256)])
            heads_v[2 * n] = y[:, :128].astype(BF16)
            heads_v[2 * n + 1] = y[:, 128:].astype(BF16)
            back1[c][:, pl.ds(pl.multiple_of(t * 128, 128), 128)] = pair_rows(
                y[:, :128], y[:, 128:]
            ).astype(BF16)
            return carry

        lax.fori_loop(0, BACK_TILES[c], project, 0)
        by_row.start(back1[c], back1_in[c], b1s.at[c], b1r.at[c])

    loads[3].wait()

    def pass_back(c):
        by_row.arrived(back1[c], back1_in[c], b1s.at[c], b1r.at[c])
        turned = dot(turn, back1_in[c][...]).astype(BF16)
        for t in range(BACK_TILES[c]):
            back2[c][:, t * 256 : t * 256 + 128] = turned[:N, t * 128 : (t + 1) * 128]
            back2[c][:, t * 256 + 128 : (t + 1) * 256] = turned[N:, t * 128 : (t + 1) * 128]
        by_col.start(back2[c], back_in[c], b2s.at[c], b2r.at[c])

    def masked(source, g, masks):
        return jnp.concatenate(
            [
                jnp.concatenate([source[g * GROUP + h] * mask for mask in masks], axis=1)
                for h in range(GROUP)
            ],
            axis=0,
        )

    pair_id = jnp.floor(local_id * 0.5)
    second = local_id != pair_id * 2.0

    def masks_of(k):
        return [one_zero(pair_id == (PAIRS * k + i).astype(F32)) for i in range(PAIRS)]

    def add_heads(target, g, value):
        for h in range(GROUP):
            at = (g * GROUP + h) * 2 * DH
            target[:, at : at + 2 * DH] += value[h * N : (h + 1) * N]

    def blocks_of(k, kind, g, side, axis):
        return jnp.concatenate(
            [blocks_v[2 * (PAIRS * k + i) + side, kind, g] for i in range(PAIRS)], axis=axis
        )

    def score_step(k, carry):
        masks = masks_of(k)
        for g in range(2):
            keys = jnp.concatenate([blocks_of(k, 0, g, side, 1) for side in range(2)], axis=0)
            add_heads(score, g, dot_t(masked(heads_v, g, masks), keys))
        return carry

    def value_step(k, carry):
        masks = masks_of(k)
        for g in range(2):
            values = jnp.concatenate([blocks_of(k, 1, g, side, 0) for side in range(2)], axis=1)
            add_heads(total, g, dot(masked(prob, g, masks), values))
        return carry

    def side_of(source, i):
        at = i * 2 * DH
        return jnp.where(second, source[:, at + DH : at + 2 * DH], source[:, at : at + DH])

    lax.fori_loop(0, 1, score_step, 0)
    pass_back(0)
    lax.fori_loop(1, 2, score_step, 0)
    pass_back(1)

    for g in range(2):
        stats = jnp.zeros((N, N), F32)
        for h in range(GROUP):
            s = side_of(score, g * GROUP + h) * SCORE_SCALE
            top = jnp.max(s, axis=1, keepdims=True)
            e = jnp.exp2(s - top)
            prob[g * GROUP + h] = e.astype(BF16)
            stats = jnp.where(along == h, top, stats)
            stats = jnp.where(along == 8 + h, jnp.sum(e, axis=1, keepdims=True), stats)
        stat[g] = stats

    lax.fori_loop(0, 1, value_step, 0)
    pass_back(2)
    lax.fori_loop(1, 2, value_step, 0)

    for c in range(SHARE_CHUNKS):
        for b in range(4):
            h = c * 4 + b
            sides = []
            for g in range(2):
                stats = stat[g]
                if h < GROUP:
                    sides.append(side_of(total, g * GROUP + h) / stats[:, 8 + h : 9 + h])
                else:
                    high = stats.astype(BF16).astype(F32)
                    rest = stats - high
                    middle = rest.astype(BF16).astype(F32)
                    low = rest - middle
                    sides.append(
                        high + pltpu.roll(middle, shift=16, axis=1) + pltpu.roll(low, shift=32, axis=1)
                    )
            share1[c, :, b * 128 : (b + 1) * 128] = pair_rows(sides[0], sides[1]).astype(BF16)
        by_row.start(share1.at[c], share1_in.at[c], s1s.at[c], s1r.at[c])

    def take_back(c):
        by_col.arrived(back2[c], back_in[c], b2s.at[c], b2r.at[c])
        own = dot(unsort, back_in[c][...]).astype(BF16)
        for t in range(BACK_TILES[c]):
            n = BACK_STARTS[c] + t
            if n < GROUP:
                for half in range(2):
                    store_query(2 * n + half, slice(0, DH), own[:, t * 256 + half * 128 :][:, :DH])
            else:
                kv_v[:, (n - GROUP) * 256 : (n - GROUP + 1) * 256] = own[
                    :, t * 256 : (t + 1) * 256
                ]

    take_back(0)
    loads[4].wait()
    spans = [slice(k, k + KEYS) for k in range(0, prefix_v.shape[2], KEYS)]
    ones = jnp.ones((KEYS, DH), BF16)

    def near_scores(q, g, span, top):
        keys = jnp.concatenate([prefix_v[0, g, span], block_v[span]], axis=1)
        part = dot_t(q, keys)
        near_score[:, span] = part
        for w in range(KEYS // 128):
            top = jnp.maximum(top, part[:, w * 128 : (w + 1) * 128])
        return top

    def near_values(top, g, span, sums):
        e = jnp.exp2(near_score[:, span] * SCORE_SCALE - top).astype(BF16)
        return sums + dot(e, jnp.concatenate([prefix_v[1, g, span], ones], axis=1))

    def keep_top(t, top):
        near_top[t] = jnp.broadcast_to(
            jnp.max(top, axis=1, keepdims=True) * SCORE_SCALE, (TILE, DH)
        )

    def tile(t, carry):
        later = t + 1
        q = query_v[later]
        top = near_top[t][:, :1]
        next_top = jnp.full((TILE, DH), EXCLUDED, F32)
        sums = jnp.zeros((TILE, 2 * DH), F32)
        for span in spans:
            sums = near_values(top, t // 2, span, sums)
            next_top = near_scores(q, later // 2, span, next_top)
        near_total[t] = sums
        keep_top(later, next_top)
        return carry

    first_top = jnp.full((TILE, DH), EXCLUDED, F32)
    for span in spans:
        first_top = near_scores(query_v[0], 0, span, first_top)
    keep_top(0, first_top)
    lax.fori_loop(0, 1, tile, 0)
    take_back(1)

    for c in range(SHARE_CHUNKS):
        by_row.arrived(share1.at[c], share1_in.at[c], s1s.at[c], s1r.at[c])
        turned = dot(turn, share1_in[c]).astype(BF16)
        share2[c, :, :512] = turned[:N]
        share2[c, :, 512:] = turned[N:]
        by_col.start(share2.at[c], share_in.at[c], s2s.at[c], s2r.at[c])

    lax.fori_loop(1, TILES - 1, tile, 0)
    take_back(2)
    save_kv = pltpu.make_async_copy(kv_v, kv_ref, save_sem.at[2])
    save_kv.start()
    last_top = near_top[TILES - 1][:, :1]
    last_sums = jnp.zeros((TILE, 2 * DH), F32)
    for span in spans:
        last_sums = near_values(last_top, 1, span, last_sums)
    near_total[TILES - 1] = last_sums

    for c in range(SHARE_CHUNKS):
        by_col.arrived(share2.at[c], share_in.at[c], s2s.at[c], s2r.at[c])
    saves = [save_kv]
    for g in range(2):
        packed = dot(unsort, share_in[1, :, g * 512 + 384 : g * 512 + 512])
        stats = (
            packed
            + pltpu.roll(packed, shift=N - 16, axis=1)
            + pltpu.roll(packed, shift=N - 32, axis=1)
        )
        for h in range(GROUP):
            c, b = h // 4, h % 4
            i = g * GROUP + h
            part = dot(unsort, share_in[c, :, g * 512 + b * 128 : g * 512 + (b + 1) * 128])
            top_far = stats[:, h : h + 1]
            mass_far = stats[:, 8 + h : 9 + h]
            rows = slice(h * SIDE, (h + 1) * SIDE)
            top_near = jnp.concatenate([near_top[2 * g, rows], near_top[2 * g + 1, rows]], axis=0)
            top = jnp.maximum(top_near, top_far)
            near = jnp.exp2(top_near - top)
            far = jnp.exp2(top_far - top) * mass_far
            sums = jnp.concatenate([near_total[2 * g, rows], near_total[2 * g + 1, rows]], axis=0)
            whole = sums[:, DH:] * near + far
            context_v[:, i * DH : (i + 1) * DH] = (
                (sums[:, :DH] * near + part * far) / whole
            ).astype(BF16)

        lanes = pl.ds(g * GROUP * DH, GROUP * DH)
        save = pltpu.make_async_copy(
            context_v.at[:, lanes], context_ref.at[:, lanes], save_sem.at[g]
        )
        save.start()
        saves.append(save)

    by_col.sent(id_out1, id_in1, i1s, i1r)
    by_row8.sent(id_out2, id_in2, i2s, i2r)
    for c in range(DELTA_CHUNKS):
        by_col.sent(out1[c], in1[c], d1s.at[c], d1r.at[c])
        by_row.sent(out2[c], in2[c], d2s.at[c], d2r.at[c])
    for c in range(BACK_CHUNKS):
        by_row.sent(back1[c], back1_in[c], b1s.at[c], b1r.at[c])
        by_col.sent(back2[c], back_in[c], b2s.at[c], b2r.at[c])
    for c in range(SHARE_CHUNKS):
        by_row.sent(share1.at[c], share1_in.at[c], s1s.at[c], s1r.at[c])
        by_col.sent(share2.at[c], share_in.at[c], s2s.at[c], s2r.at[c])
    for save in saves:
        save.wait()


def result_kernel(context_in, kv_in, context_ref, kv_ref, context_v, kv_v, sem):
    top, bottom = pl.ds(0, SIDE), pl.ds(SIDE, SIDE)
    hops = [
        (context_in.at[top], context_v.at[top], context_ref.at[top]),
        (context_in.at[bottom], context_v.at[bottom], context_ref.at[bottom]),
        (kv_in, kv_v, kv_ref),
    ]
    fetches = [pltpu.make_async_copy(h[0], h[1], sem.at[0, i]) for i, h in enumerate(hops)]
    stores = [pltpu.make_async_copy(h[1], h[2], sem.at[1, i]) for i, h in enumerate(hops)]
    for fetch in fetches:
        fetch.start()
    for fetch, store in zip(fetches, stores):
        fetch.wait()
        store.start()
    for store in stores:
        store.wait()


def local(
    child_parent,
    prefix_len,
    child_delta,
    parent_hidden,
    parent_cache,
    prefix_cache,
    norm_gain,
    w_query,
    w_kv,
):
    vmem = pl.BlockSpec(memory_space=pltpu.VMEM)
    hbm = pl.BlockSpec(memory_space=pl.ANY)
    dma = pltpu.SemaphoreType.DMA
    ids = child_parent.reshape(1, N)
    lens = prefix_len.reshape(1, N)
    tokens = prefix_cache.shape[3]
    share_shape = (SHARE_CHUNKS, N, 1024)
    results = (
        jax.ShapeDtypeStruct((N, HEADS * DH), BF16),
        jax.ShapeDtypeStruct((N, 512), BF16),
    )
    context, new_kv = pl.pallas_call(
        layer_kernel,
        name="decode_layer",
        out_shape=results,
        in_specs=[vmem, vmem, vmem, hbm, hbm, hbm, hbm, hbm, hbm],
        out_specs=(hbm, hbm),
        scratch_shapes=[
            pltpu.VMEM((N, D), BF16),
            pltpu.VMEM((PARENTS, D), BF16),
            pltpu.VMEM((PARENTS, 2, 2, BLOCK, DH), BF16),
            pltpu.VMEM((D, 2304), BF16),
            [pltpu.VMEM((N, 2 * half), BF16) for half in DELTA_HALVES],
            [pltpu.VMEM((N, 2 * half), BF16) for half in DELTA_HALVES],
            [pltpu.VMEM((2 * N, half), BF16) for half in DELTA_HALVES],
            [pltpu.VMEM((2 * N, half), BF16) for half in DELTA_HALVES],
            pltpu.VMEM((N, N), BF16),
            pltpu.VMEM((N, N), BF16),
            pltpu.VMEM((N, N), F32),
            pltpu.VMEM((N, N), F32),
            pltpu.VMEM((N, D), BF16),
            pltpu.VMEM((18, N, 128), BF16),
            [pltpu.VMEM((2 * N, tiles * 128), BF16) for tiles in BACK_TILES],
            [pltpu.VMEM((2 * N, tiles * 128), BF16) for tiles in BACK_TILES],
            [pltpu.VMEM((N, tiles * 256), BF16) for tiles in BACK_TILES],
            pltpu.VMEM((HEADS, N, BLOCK), BF16),
            pltpu.VMEM((2, N, N), F32),
            pltpu.VMEM((SHARE_CHUNKS, 2 * N, 512), BF16),
            pltpu.VMEM((SHARE_CHUNKS, 2 * N, 512), BF16),
            pltpu.VMEM(share_shape, BF16),
            [pltpu.VMEM((N, tiles * 256), BF16) for tiles in BACK_TILES],
            pltpu.VMEM(share_shape, BF16),
            pltpu.VMEM((2, 2, tokens, DH), BF16),
            pltpu.VMEM((tokens, BLOCK), BF16),
            pltpu.VMEM((TILES, TILE, 2 * DH), BF16),
            pltpu.VMEM((TILE, tokens), F32),
            pltpu.VMEM((TILES, TILE, 2 * DH), F32),
            pltpu.VMEM((TILES, TILE, DH), F32),
            pltpu.VMEM((N, 512), BF16),
            pltpu.VMEM((N, HEADS * DH), BF16),
            dma((3,)),
            dma((6,)),
            dma((DELTA_CHUNKS,)),
            dma((DELTA_CHUNKS,)),
            dma((DELTA_CHUNKS,)),
            dma((DELTA_CHUNKS,)),
            dma(()),
            dma(()),
            dma(()),
            dma(()),
            dma((BACK_CHUNKS,)),
            dma((BACK_CHUNKS,)),
            dma((BACK_CHUNKS,)),
            dma((BACK_CHUNKS,)),
            dma((SHARE_CHUNKS,)),
            dma((SHARE_CHUNKS,)),
            dma((SHARE_CHUNKS,)),
            dma((SHARE_CHUNKS,)),
        ],
        compiler_params=pltpu.CompilerParams(
            collective_id=0, has_side_effects=True, vmem_limit_bytes=60 << 20
        ),
    )(
        ids,
        lens,
        norm_gain.reshape(D // 128, 128),
        child_delta,
        parent_hidden,
        parent_cache,
        w_query,
        w_kv,
        prefix_cache.reshape(prefix_cache.shape[1:]),
    )
    return pl.pallas_call(
        result_kernel,
        name="results",
        out_shape=results,
        in_specs=[hbm, hbm],
        out_specs=(hbm, hbm),
        scratch_shapes=[
            pltpu.VMEM((N, HEADS * DH), BF16),
            pltpu.VMEM((N, 512), BF16),
            dma((2, 3)),
        ],
        compiler_params=pltpu.CompilerParams(vmem_limit_bytes=60 << 20),
    )(context, new_kv)


def solution(mesh):
    return jax.shard_map(
        local,
        mesh=mesh,
        in_specs=(
            P(("row", "col")),
            P(("row", "col")),
            P(("row", "col"), None),
            P(("row", "col"), None),
            P(("row", "col"), None, None, None, None),
            P(("row", "col"), None, None, None, None),
            P(),
            P(),
            P(),
        ),
        out_specs=(P(("row", "col"), None), P(("row", "col"), None)),
        check_vma=False,
    )
```

```python
import math

import jax
import jax.numpy as jnp
from jax import lax
from jax.experimental import pallas as pl
from jax.experimental.pallas import tpu as pltpu
from jax.sharding import PartitionSpec as P

EPSILON = 1e-06
F32 = jnp.float32
BF16 = jnp.bfloat16
I32 = jnp.int32
ROWS = 16
COLS = 8
N = 128
D = 3584
HEADS = 14
GROUP = 7
DH = 128
PARENTS = 32
BLOCK = 128
DELTA_HALVES = (512, 512, 384, 384)
DELTA_STARTS = (0, 1024, 2048, 2816)
DELTA_CHUNKS = 4
BACK_TILES = (4, 3, 2)
BACK_STARTS = (0, 4, 7)
BACK_CHUNKS = 3
SHARE_CHUNKS = 2
KEYS = 512
TILES = 4
TILE = GROUP * N * 2 // TILES
PAIRS = 8
SIDE = N // 2
EXCLUDED = -1e30
SCORE_SCALE = math.log2(math.e) / math.sqrt(DH)


def iotas(shape):
    return lax.broadcasted_iota(I32, shape, 0), lax.broadcasted_iota(I32, shape, 1)


def one_zero(mask, kind=BF16):
    return jnp.where(mask, 1.0, 0.0).astype(kind)


def to_col(row):
    below, along = iotas((N, N))
    return jnp.sum(jnp.where(below == along, row, 0.0), axis=1, keepdims=True)


def to_row(col):
    below, along = iotas((N, N))
    return jnp.sum(jnp.where(below == along, col, 0.0), axis=0, keepdims=True)


def rank_row(key_row, key_col):
    below, along = iotas((N, N))
    earlier = (key_col == key_row) & (below < along)
    return jnp.sum(jnp.where(earlier, 1.0, 0.0), axis=0, keepdims=True)


def column_order(ids):
    column = ((ids >> 5) & (COLS - 1)).astype(F32)
    return column * 16.0 + rank_row(column, to_col(column))


def dot(a, b):
    return jnp.dot(a, b, preferred_element_type=F32)


def dot_t(a, b):
    return lax.dot_general(a, b, (((1,), (1,)), ((), ())), preferred_element_type=F32)


def pair_rows(left, right):
    width = left.shape[1]
    both = jnp.concatenate(
        [left.reshape(ROWS, 1, 8, width), right.reshape(ROWS, 1, 8, width)], axis=1
    )
    return both.reshape(2 * N, width)


class Exchange:
    def __init__(self, axis, count, me, rows):
        self.axis, self.count, self.me, self.rows = axis, count, me, rows

    def part(self, ref, k):
        return ref.at[pl.ds(pl.multiple_of(k * self.rows, self.rows), self.rows)]

    def copy(self, src, dst, send, recv, k, slot):
        return pltpu.make_async_remote_copy(
            src_ref=self.part(src, k),
            dst_ref=self.part(dst, slot),
            send_sem=send,
            recv_sem=recv,
            device_id={self.axis: k},
            device_id_type=pl.DeviceIdType.MESH,
        )

    def whole(self, src, dst, send, recv):
        rows = pl.ds(0, (self.count - 1) * self.rows)
        return pltpu.make_async_remote_copy(
            src_ref=src.at[rows],
            dst_ref=dst.at[rows],
            send_sem=send,
            recv_sem=recv,
            device_id={self.axis: lax.rem(self.me + 1, self.count)},
            device_id_type=pl.DeviceIdType.MESH,
        )

    def start(self, src, dst, send, recv):
        def body(k, carry):
            self.copy(src, dst, send, recv, lax.rem(self.me + k, self.count), self.me).start()
            return carry

        lax.fori_loop(1, self.count, body, 0)
        own = pl.ds(pl.multiple_of(self.me * self.rows, self.rows), self.rows)
        dst[own, :] = src[own, :]

    def arrived(self, src, dst, send, recv):
        self.whole(src, dst, send, recv).wait_recv()

    def sent(self, src, dst, send, recv):
        self.whole(src, dst, send, recv).wait_send()


def layer_kernel(
    ids_ref,
    lens_ref,
    gain_ref,
    delta_hbm,
    hidden_hbm,
    blocks_hbm,
    wq_hbm,
    wkv_hbm,
    prefix_hbm,
    context_ref,
    kv_ref,
    delta_v,
    hidden_v,
    blocks_v,
    weight_v,
    out1,
    in1,
    out2,
    in2,
    id_out1,
    id_in1,
    id_out2,
    id_in2,
    normed,
    heads_v,
    back1,
    back1_in,
    back2,
    prob,
    stat,
    share1,
    share1_in,
    share2,
    back_in,
    share_in,
    prefix_v,
    block_v,
    query_v,
    near_score,
    near_total,
    near_top,
    kv_v,
    context_v,
    save_sem,
    load_sem,
    d1s,
    d1r,
    d2s,
    d2r,
    i1s,
    i1r,
    i2s,
    i2r,
    b1s,
    b1r,
    b2s,
    b2r,
    s1s,
    s1r,
    s2s,
    s2r,
):
    my_row = lax.axis_index("row")
    my_col = lax.axis_index("col")
    load_delta = pltpu.make_async_copy(delta_hbm, delta_v, load_sem.at[0])
    load_delta.start()

    barrier = pltpu.get_barrier_semaphore()

    def greet_col(k, carry):
        pl.semaphore_signal(
            barrier,
            inc=1,
            device_id={"col": lax.rem(my_col + k, COLS)},
            device_id_type=pl.DeviceIdType.MESH,
        )
        return carry

    def greet_row(k, carry):
        pl.semaphore_signal(
            barrier,
            inc=1,
            device_id={"row": lax.rem(my_row + k, ROWS)},
            device_id_type=pl.DeviceIdType.MESH,
        )
        return carry

    lax.fori_loop(1, COLS, greet_col, 0)
    lax.fori_loop(1, ROWS, greet_row, 0)

    below, along = iotas((N, N))
    ids = ids_ref[...]
    order = column_order(ids)
    pick = order == below.astype(F32)
    sorting = one_zero(pick)
    far_row = (ids >> 8).astype(F32)
    far_local = (ids & (PARENTS - 1)).astype(F32)
    row_sorted = jnp.sum(jnp.where(pick, far_row, 0.0), axis=1, keepdims=True)
    local_sorted = jnp.sum(jnp.where(pick, far_local, 0.0), axis=1, keepdims=True)
    id_out1[...] = jnp.where(along < 64, row_sorted, local_sorted).astype(BF16)

    loads = [
        pltpu.make_async_copy(hidden_hbm, hidden_v, load_sem.at[1]),
        pltpu.make_async_copy(wq_hbm, weight_v.at[:, pl.ds(0, HEADS * DH)], load_sem.at[2]),
        pltpu.make_async_copy(wkv_hbm, weight_v.at[:, pl.ds(HEADS * DH, 512)], load_sem.at[3]),
        pltpu.make_async_copy(blocks_hbm, blocks_v, load_sem.at[4]),
        pltpu.make_async_copy(prefix_hbm, prefix_v, load_sem.at[5]),
    ]
    load_delta.wait()
    for load in loads:
        load.start()
    order_col = to_col(order)
    unsort = one_zero(order_col == along.astype(F32))
    lens_col = to_col(lens_ref[...].astype(F32))
    bias = jnp.where(along.astype(F32) < lens_col, 0.0, EXCLUDED).astype(BF16)

    by_col = Exchange("col", COLS, my_col, 16)
    by_row = Exchange("row", ROWS, my_row, 16)
    by_row8 = Exchange("row", ROWS, my_row, 8)

    pl.semaphore_wait(barrier, COLS + ROWS - 2)
    by_col.start(id_out1, id_in1, i1s, i1r)
    for c in range(DELTA_CHUNKS):
        first = DELTA_STARTS[c]
        out1[c][...] = dot(sorting, delta_v[:, first : first + 2 * DELTA_HALVES[c]]).astype(BF16)
        by_col.start(out1[c], in1[c], d1s.at[c], d1r.at[c])

    wide = near_score.at[0:N, 0:D]
    score = near_score.at[N : 2 * N, 0 : 2 * HEADS * DH]
    total = near_score.at[2 * N : 3 * N, 0 : 2 * HEADS * DH]
    score[...] = jnp.zeros(score.shape, F32)
    total[...] = jnp.zeros(total.shape, F32)
    def store_query(h, lanes, value):
        at = (h % GROUP) * SIDE
        for side in range(2):
            query_v[(h // GROUP) * 2 + side, at : at + SIDE, lanes] = value[
                side * SIDE : (side + 1) * SIDE
            ]

    for h in range(HEADS):
        store_query(h, slice(DH, 2 * DH), bias)
    for b in range(prefix_v.shape[2] // BLOCK):
        block_v[b * BLOCK : (b + 1) * BLOCK] = one_zero(along == b)

    by_col.arrived(id_out1, id_in1, i1s, i1r)
    arrived_ids = id_in1[...].astype(F32)
    row_col = arrived_ids[:, 0:1]
    row_row = to_row(row_col)
    local_row = to_row(arrived_ids[:, 64:65])
    place = row_row * 8.0 + rank_row(row_row, row_col)
    place_col = to_col(place)
    place_pick = place == below.astype(F32)
    id_out2[...] = jnp.broadcast_to(
        jnp.sum(jnp.where(place_pick, local_row, 0.0), axis=1, keepdims=True), (N, N)
    )
    by_row8.start(id_out2, id_in2, i2s, i2r)

    wide_below, wide_along = iotas((2 * N, 2 * N))
    code_below = ((wide_below >> 4) * 16 + (wide_below & 7) * 2 + ((wide_below >> 3) & 1)).astype(
        F32
    )
    code_along = ((wide_along >> 4) * 16 + (wide_along & 7) * 2 + ((wide_along >> 3) & 1)).astype(
        F32
    )
    code_row = jnp.concatenate([place * 2.0, place * 2.0 + 1.0], axis=1)
    code_col = jnp.concatenate([place_col * 2.0, place_col * 2.0 + 1.0], axis=0)
    forth = one_zero(code_below == code_row)
    turn = one_zero(code_along == code_col)

    for c in range(DELTA_CHUNKS):
        by_col.arrived(out1[c], in1[c], d1s.at[c], d1r.at[c])
        width = DELTA_HALVES[c]
        stacked = jnp.concatenate([in1[c][:, :width], in1[c][:, width:]], axis=0)
        out2[c][...] = dot(forth, stacked).astype(BF16)
        by_row.start(out2[c], in2[c], d2s.at[c], d2r.at[c])

    loads[0].wait()
    by_row8.arrived(id_out2, id_in2, i2s, i2r)
    local_id = id_in2[...]
    owner = one_zero(local_id[:, :PARENTS] == along[:, :PARENTS].astype(F32))
    squares = jnp.zeros((N, 1), F32)
    for c in range(DELTA_CHUNKS):
        by_row.arrived(out2[c], in2[c], d2s.at[c], d2r.at[c])
        for half in range(2):
            for w in range(DELTA_HALVES[c] // 128):
                at = DELTA_STARTS[c] + half * DELTA_HALVES[c] + w * 128
                grid = in2[c][:, w * 128 : (w + 1) * 128].astype(F32)
                grid = grid.reshape(ROWS, 2, 8, 128)[:, half].reshape(N, 128)
                value = dot(owner, hidden_v[:, at : at + 128]) + grid
                wide[:, at : at + 128] = value
                squares = squares + jnp.sum(value * value, axis=1, keepdims=True)
    inverse = lax.rsqrt(squares / D + EPSILON)
    for w in range(D // 128):
        at = w * 128
        normed[:, at : at + 128] = (
            wide[:, at : at + 128] * inverse * gain_ref[w : w + 1]
        ).astype(BF16)

    loads[1].wait()
    loads[2].wait()
    for c in range(BACK_CHUNKS):

        def project(t, carry, c=c):
            n = BACK_STARTS[c] + t
            y = dot(normed[...], weight_v[:, pl.ds(pl.multiple_of(n * 256, 256), 256)])
            heads_v[2 * n] = y[:, :128].astype(BF16)
            heads_v[2 * n + 1] = y[:, 128:].astype(BF16)
            back1[c][:, pl.ds(pl.multiple_of(t * 128, 128), 128)] = pair_rows(
                y[:, :128], y[:, 128:]
            ).astype(BF16)
            return carry

        lax.fori_loop(0, BACK_TILES[c], project, 0)
        by_row.start(back1[c], back1_in[c], b1s.at[c], b1r.at[c])

    loads[3].wait()

    def pass_back(c):
        by_row.arrived(back1[c], back1_in[c], b1s.at[c], b1r.at[c])
        turned = dot(turn, back1_in[c][...]).astype(BF16)
        for t in range(BACK_TILES[c]):
            back2[c][:, t * 256 : t * 256 + 128] = turned[:N, t * 128 : (t + 1) * 128]
            back2[c][:, t * 256 + 128 : (t + 1) * 256] = turned[N:, t * 128 : (t + 1) * 128]
        by_col.start(back2[c], back_in[c], b2s.at[c], b2r.at[c])

    def masked(source, g, masks):
        return jnp.concatenate(
            [
                jnp.concatenate([source[g * GROUP + h] * mask for mask in masks], axis=1)
                for h in range(GROUP)
            ],
            axis=0,
        )

    pair_id = jnp.floor(local_id * 0.5)
    second = local_id != pair_id * 2.0

    def masks_of(k):
        return [one_zero(pair_id == (PAIRS * k + i).astype(F32)) for i in range(PAIRS)]

    def add_heads(target, g, value):
        for h in range(GROUP):
            at = (g * GROUP + h) * 2 * DH
            target[:, at : at + 2 * DH] += value[h * N : (h + 1) * N]

    def blocks_of(k, kind, g, side, axis):
        return jnp.concatenate(
            [blocks_v[2 * (PAIRS * k + i) + side, kind, g] for i in range(PAIRS)], axis=axis
        )

    def score_step(k, carry):
        masks = masks_of(k)
        for g in range(2):
            keys = jnp.concatenate([blocks_of(k, 0, g, side, 1) for side in range(2)], axis=0)
            add_heads(score, g, dot_t(masked(heads_v, g, masks), keys))
        return carry

    def value_step(k, carry):
        masks = masks_of(k)
        for g in range(2):
            values = jnp.concatenate([blocks_of(k, 1, g, side, 0) for side in range(2)], axis=1)
            add_heads(total, g, dot(masked(prob, g, masks), values))
        return carry

    def side_of(source, i):
        at = i * 2 * DH
        return jnp.where(second, source[:, at + DH : at + 2 * DH], source[:, at : at + DH])

    lax.fori_loop(0, 1, score_step, 0)
    pass_back(0)
    lax.fori_loop(1, 2, score_step, 0)
    pass_back(1)

    for g in range(2):
        stats = jnp.zeros((N, N), F32)
        for h in range(GROUP):
            s = side_of(score, g * GROUP + h) * SCORE_SCALE
            top = jnp.max(s, axis=1, keepdims=True)
            e = jnp.exp2(s - top)
            prob[g * GROUP + h] = e.astype(BF16)
            stats = jnp.where(along == h, top, stats)
            stats = jnp.where(along == 8 + h, jnp.sum(e, axis=1, keepdims=True), stats)
        stat[g] = stats

    lax.fori_loop(0, 2, value_step, 0)

    for c in range(SHARE_CHUNKS):
        for b in range(4):
            h = c * 4 + b
            sides = []
            for g in range(2):
                stats = stat[g]
                if h < GROUP:
                    sides.append(side_of(total, g * GROUP + h) / stats[:, 8 + h : 9 + h])
                else:
                    high = stats.astype(BF16).astype(F32)
                    rest = stats - high
                    middle = rest.astype(BF16).astype(F32)
                    low = rest - middle
                    sides.append(
                        high + pltpu.roll(middle, shift=16, axis=1) + pltpu.roll(low, shift=32, axis=1)
                    )
            share1[c, :, b * 128 : (b + 1) * 128] = pair_rows(sides[0], sides[1]).astype(BF16)
        by_row.start(share1.at[c], share1_in.at[c], s1s.at[c], s1r.at[c])

    def take_back(c):
        by_col.arrived(back2[c], back_in[c], b2s.at[c], b2r.at[c])
        own = dot(unsort, back_in[c][...]).astype(BF16)
        for t in range(BACK_TILES[c]):
            n = BACK_STARTS[c] + t
            if n < GROUP:
                for half in range(2):
                    store_query(2 * n + half, slice(0, DH), own[:, t * 256 + half * 128 :][:, :DH])
            else:
                kv_v[:, (n - GROUP) * 256 : (n - GROUP + 1) * 256] = own[
                    :, t * 256 : (t + 1) * 256
                ]

    take_back(0)
    loads[4].wait()
    spans = [slice(k, k + KEYS) for k in range(0, prefix_v.shape[2], KEYS)]
    ones = jnp.ones((KEYS, DH), BF16)

    def near_scores(q, g, span, top):
        keys = jnp.concatenate([prefix_v[0, g, span], block_v[span]], axis=1)
        part = dot_t(q, keys)
        near_score[:, span] = part
        for w in range(KEYS // 128):
            top = jnp.maximum(top, part[:, w * 128 : (w + 1) * 128])
        return top

    def near_values(top, g, span, sums):
        e = jnp.exp2(near_score[:, span] * SCORE_SCALE - top).astype(BF16)
        return sums + dot(e, jnp.concatenate([prefix_v[1, g, span], ones], axis=1))

    def keep_top(t, top):
        near_top[t] = jnp.broadcast_to(
            jnp.max(top, axis=1, keepdims=True) * SCORE_SCALE, (TILE, DH)
        )

    def tile(t, carry):
        later = t + 1
        q = query_v[later]
        top = near_top[t][:, :1]
        next_top = jnp.full((TILE, DH), EXCLUDED, F32)
        sums = jnp.zeros((TILE, 2 * DH), F32)
        for span in spans:
            sums = near_values(top, t // 2, span, sums)
            next_top = near_scores(q, later // 2, span, next_top)
        near_total[t] = sums
        keep_top(later, next_top)
        return carry

    first_top = jnp.full((TILE, DH), EXCLUDED, F32)
    for span in spans:
        first_top = near_scores(query_v[0], 0, span, first_top)
    keep_top(0, first_top)
    pass_back(2)
    lax.fori_loop(0, 1, tile, 0)
    take_back(1)

    for c in range(SHARE_CHUNKS):
        by_row.arrived(share1.at[c], share1_in.at[c], s1s.at[c], s1r.at[c])
        turned = dot(turn, share1_in[c]).astype(BF16)
        share2[c, :, :512] = turned[:N]
        share2[c, :, 512:] = turned[N:]
        by_col.start(share2.at[c], share_in.at[c], s2s.at[c], s2r.at[c])

    lax.fori_loop(1, TILES - 1, tile, 0)
    take_back(2)
    save_kv = pltpu.make_async_copy(kv_v, kv_ref, save_sem.at[2])
    save_kv.start()
    last_top = near_top[TILES - 1][:, :1]
    last_sums = jnp.zeros((TILE, 2 * DH), F32)
    for span in spans:
        last_sums = near_values(last_top, 1, span, last_sums)
    near_total[TILES - 1] = last_sums

    for c in range(SHARE_CHUNKS):
        by_col.arrived(share2.at[c], share_in.at[c], s2s.at[c], s2r.at[c])
    saves = [save_kv]
    for g in range(2):
        packed = dot(unsort, share_in[1, :, g * 512 + 384 : g * 512 + 512])
        stats = (
            packed
            + pltpu.roll(packed, shift=N - 16, axis=1)
            + pltpu.roll(packed, shift=N - 32, axis=1)
        )
        for h in range(GROUP):
            c, b = h // 4, h % 4
            i = g * GROUP + h
            part = dot(unsort, share_in[c, :, g * 512 + b * 128 : g * 512 + (b + 1) * 128])
            top_far = stats[:, h : h + 1]
            mass_far = stats[:, 8 + h : 9 + h]
            rows = slice(h * SIDE, (h + 1) * SIDE)
            top_near = jnp.concatenate([near_top[2 * g, rows], near_top[2 * g + 1, rows]], axis=0)
            top = jnp.maximum(top_near, top_far)
            near = jnp.exp2(top_near - top)
            far = jnp.exp2(top_far - top) * mass_far
            sums = jnp.concatenate([near_total[2 * g, rows], near_total[2 * g + 1, rows]], axis=0)
            whole = sums[:, DH:] * near + far
            context_v[:, i * DH : (i + 1) * DH] = (
                (sums[:, :DH] * near + part * far) / whole
            ).astype(BF16)

        lanes = pl.ds(g * GROUP * DH, GROUP * DH)
        save = pltpu.make_async_copy(
            context_v.at[:, lanes], context_ref.at[:, lanes], save_sem.at[g]
        )
        save.start()
        saves.append(save)

    by_col.sent(id_out1, id_in1, i1s, i1r)
    by_row8.sent(id_out2, id_in2, i2s, i2r)
    for c in range(DELTA_CHUNKS):
        by_col.sent(out1[c], in1[c], d1s.at[c], d1r.at[c])
        by_row.sent(out2[c], in2[c], d2s.at[c], d2r.at[c])
    for c in range(BACK_CHUNKS):
        by_row.sent(back1[c], back1_in[c], b1s.at[c], b1r.at[c])
        by_col.sent(back2[c], back_in[c], b2s.at[c], b2r.at[c])
    for c in range(SHARE_CHUNKS):
        by_row.sent(share1.at[c], share1_in.at[c], s1s.at[c], s1r.at[c])
        by_col.sent(share2.at[c], share_in.at[c], s2s.at[c], s2r.at[c])
    for save in saves:
        save.wait()


def result_kernel(context_in, kv_in, context_ref, kv_ref, context_v, kv_v, sem):
    top, bottom = pl.ds(0, SIDE), pl.ds(SIDE, SIDE)
    hops = [
        (context_in.at[top], context_v.at[top], context_ref.at[top]),
        (context_in.at[bottom], context_v.at[bottom], context_ref.at[bottom]),
        (kv_in, kv_v, kv_ref),
    ]
    fetches = [pltpu.make_async_copy(h[0], h[1], sem.at[0, i]) for i, h in enumerate(hops)]
    stores = [pltpu.make_async_copy(h[1], h[2], sem.at[1, i]) for i, h in enumerate(hops)]
    for fetch in fetches:
        fetch.start()
    for fetch, store in zip(fetches, stores):
        fetch.wait()
        store.start()
    for store in stores:
        store.wait()


def local(
    child_parent,
    prefix_len,
    child_delta,
    parent_hidden,
    parent_cache,
    prefix_cache,
    norm_gain,
    w_query,
    w_kv,
):
    vmem = pl.BlockSpec(memory_space=pltpu.VMEM)
    hbm = pl.BlockSpec(memory_space=pl.ANY)
    dma = pltpu.SemaphoreType.DMA
    ids = child_parent.reshape(1, N)
    lens = prefix_len.reshape(1, N)
    tokens = prefix_cache.shape[3]
    share_shape = (SHARE_CHUNKS, N, 1024)
    results = (
        jax.ShapeDtypeStruct((N, HEADS * DH), BF16),
        jax.ShapeDtypeStruct((N, 512), BF16),
    )
    context, new_kv = pl.pallas_call(
        layer_kernel,
        name="decode_layer",
        out_shape=results,
        in_specs=[vmem, vmem, vmem, hbm, hbm, hbm, hbm, hbm, hbm],
        out_specs=(hbm, hbm),
        scratch_shapes=[
            pltpu.VMEM((N, D), BF16),
            pltpu.VMEM((PARENTS, D), BF16),
            pltpu.VMEM((PARENTS, 2, 2, BLOCK, DH), BF16),
            pltpu.VMEM((D, 2304), BF16),
            [pltpu.VMEM((N, 2 * half), BF16) for half in DELTA_HALVES],
            [pltpu.VMEM((N, 2 * half), BF16) for half in DELTA_HALVES],
            [pltpu.VMEM((2 * N, half), BF16) for half in DELTA_HALVES],
            [pltpu.VMEM((2 * N, half), BF16) for half in DELTA_HALVES],
            pltpu.VMEM((N, N), BF16),
            pltpu.VMEM((N, N), BF16),
            pltpu.VMEM((N, N), F32),
            pltpu.VMEM((N, N), F32),
            pltpu.VMEM((N, D), BF16),
            pltpu.VMEM((18, N, 128), BF16),
            [pltpu.VMEM((2 * N, tiles * 128), BF16) for tiles in BACK_TILES],
            [pltpu.VMEM((2 * N, tiles * 128), BF16) for tiles in BACK_TILES],
            [pltpu.VMEM((N, tiles * 256), BF16) for tiles in BACK_TILES],
            pltpu.VMEM((HEADS, N, BLOCK), BF16),
            pltpu.VMEM((2, N, N), F32),
            pltpu.VMEM((SHARE_CHUNKS, 2 * N, 512), BF16),
            pltpu.VMEM((SHARE_CHUNKS, 2 * N, 512), BF16),
            pltpu.VMEM(share_shape, BF16),
            [pltpu.VMEM((N, tiles * 256), BF16) for tiles in BACK_TILES],
            pltpu.VMEM(share_shape, BF16),
            pltpu.VMEM((2, 2, tokens, DH), BF16),
            pltpu.VMEM((tokens, BLOCK), BF16),
            pltpu.VMEM((TILES, TILE, 2 * DH), BF16),
            pltpu.VMEM((TILE, tokens), F32),
            pltpu.VMEM((TILES, TILE, 2 * DH), F32),
            pltpu.VMEM((TILES, TILE, DH), F32),
            pltpu.VMEM((N, 512), BF16),
            pltpu.VMEM((N, HEADS * DH), BF16),
            dma((3,)),
            dma((6,)),
            dma((DELTA_CHUNKS,)),
            dma((DELTA_CHUNKS,)),
            dma((DELTA_CHUNKS,)),
            dma((DELTA_CHUNKS,)),
            dma(()),
            dma(()),
            dma(()),
            dma(()),
            dma((BACK_CHUNKS,)),
            dma((BACK_CHUNKS,)),
            dma((BACK_CHUNKS,)),
            dma((BACK_CHUNKS,)),
            dma((SHARE_CHUNKS,)),
            dma((SHARE_CHUNKS,)),
            dma((SHARE_CHUNKS,)),
            dma((SHARE_CHUNKS,)),
        ],
        compiler_params=pltpu.CompilerParams(
            collective_id=0, has_side_effects=True, vmem_limit_bytes=60 << 20
        ),
    )(
        ids,
        lens,
        norm_gain.reshape(D // 128, 128),
        child_delta,
        parent_hidden,
        parent_cache,
        w_query,
        w_kv,
        prefix_cache.reshape(prefix_cache.shape[1:]),
    )
    return pl.pallas_call(
        result_kernel,
        name="results",
        out_shape=results,
        in_specs=[hbm, hbm],
        out_specs=(hbm, hbm),
        scratch_shapes=[
            pltpu.VMEM((N, HEADS * DH), BF16),
            pltpu.VMEM((N, 512), BF16),
            dma((2, 3)),
        ],
        compiler_params=pltpu.CompilerParams(vmem_limit_bytes=60 << 20),
    )(context, new_kv)


def solution(mesh):
    return jax.shard_map(
        local,
        mesh=mesh,
        in_specs=(
            P(("row", "col")),
            P(("row", "col")),
            P(("row", "col"), None),
            P(("row", "col"), None),
            P(("row", "col"), None, None, None, None),
            P(("row", "col"), None, None, None, None),
            P(),
            P(),
            P(),
        ),
        out_specs=(P(("row", "col"), None), P(("row", "col"), None)),
        check_vma=False,
    )
```
